256 devices in a mesh: seq: 128 (over x_lo, z, y, core), mp: 2 (over x_hi).
Axes of the slice: x: 4 (x_hi: 2, x_lo: 2; x = x_hi * 2 + x_lo), y: 4, z: 8, core: 2. Of those that a mesh axis runs over, the one named last changes fastest.
Arguments:
- patches: bfloat16 [32768, 64], P('seq'), may hold values from -6 to 6
- clip_shape: int32 [64, 3], replicated, may hold values from 1 to 16, as said below
- shard_counts: int32 [128], replicated, may hold values from 1 to 256, as said below
- patch_weight: bfloat16 [64, 2560], P(None, 'mp'), may hold values from -3 to 3
- patch_bias: float32 [2560], P('mp'), may hold values from -6 to 6
- time_mod: float32 [64, 2, 2560], P(None, None, 'mp'), may hold values from -6 to 6
- block_mod: float32 [2, 2560], P(None, 'mp'), may hold values from -4 to 4
- w_query: bfloat16 [2560, 2560], P('seq', 'mp'), may hold values from -0.47434165 to 0.47434165
- query_bias: float32 [2560], P('mp'), may hold values from -4 to 4
- w_keyvalue: bfloat16 [2560, 5120], P('seq', 'mp'), may hold values from -0.47434165 to 0.47434165
- keyvalue_bias: float32 [5120], P('mp'), may hold values from -6 to 6
- norm_gain: float32 [2, 2560], P(None, 'mp'), may hold values from 1 to 2
Outputs:
- attention: bfloat16 [32768, 2560], P('seq', 'mp')
The draws below stay inside these ranges and needn't reach their ends.
Inputs may be any that keep to these rules, and one draw needn't show every extreme that they name: `clip_shape`: clip c lies on shards 2 c to 2 c + 1. Frames run from 1 to 2, patch rows from 8 to 16, patch columns from 8 to 16; some clip has 2 frames of 16 by 16 patches. `shard_counts`: the counts of clip c's 2 shards add up to the product of clip_shape[c].
All inputs are finite; a program needn't handle non-finite values.
Results may differ from the reference program's by a relative error of at most 0.0063.
Values may be sent and summed in bfloat16 or wider, within the bound.
A program may use at most 128 MiB of HBM per device.

```python
import math
import jax
import jax.numpy as jnp
from jax import lax

D = 2560
HEADS = 20
HD = 128
CIN = 64
GROUP = 2
TOK_DEV = 256
CLIPS = 64
SLOTS = 32768


def clip_layout(key):
    base_key = jax.random.fold_in(key, 71)
    key_frames, key_height, key_width, key_pick, key_split, key_order = jax.random.split(base_key, 6)
    frames = jax.random.randint(key_frames, (CLIPS,), 1, 3)
    height = jax.random.randint(key_height, (CLIPS,), 8, 17)
    widths = jax.random.randint(key_width, (CLIPS,), TOK_DEV // 32, TOK_DEV // 16 + 1)
    chosen = jax.random.randint(key_pick, (), 0, CLIPS)
    smallest = (chosen + 1) % CLIPS
    clip_ids = jnp.arange(CLIPS)
    frames = jnp.where(clip_ids == chosen, 2, jnp.where(clip_ids == smallest, 1, frames))
    height = jnp.where(clip_ids == chosen, 16, jnp.where(clip_ids == smallest, 8, height))
    widths = jnp.where(clip_ids == chosen, TOK_DEV // 16, jnp.where(clip_ids == smallest, TOK_DEV // 32, widths))
    sizes = frames * height * widths
    share = sizes // GROUP
    spare = sizes % GROUP
    margin = jnp.maximum(jnp.minimum(TOK_DEV - share - 1, share - 1), 0)
    shifts = jax.random.randint(key_split, (CLIPS, GROUP // 2), -margin[:, None], margin[:, None] + 1)
    parts = share[:, None] + jnp.concatenate([shifts, -shifts], axis=1)
    parts = parts + jnp.where(jnp.arange(GROUP)[None, :] < spare[:, None], 1, 0)
    order_keys = jax.random.split(key_order, CLIPS)
    parts = jax.vmap(lambda one_key, one_row: jax.random.permutation(one_key, one_row))(order_keys, parts)
    shapes = jnp.stack([frames, height, widths], axis=1).astype(jnp.int32)
    return (shapes, parts.reshape(CLIPS * GROUP).astype(jnp.int32))


def draw_clip_shape(key, part):
    return clip_layout(key)[0]


def draw_shard_counts(key, part):
    return clip_layout(key)[1]


def base_values(key, rows, columns):
    return (jnp.clip(jax.random.normal(key, (rows, columns), jnp.float32), -4.0, 4.0), 3.0)


def draw_patch_weight(key, part):
    key_base, key_scale = jax.random.split(jax.random.fold_in(key, 13))
    values, ramp_base = base_values(key_base, CIN, D)
    rising = ramp_base ** (jnp.arange(D, dtype=jnp.float32) / (D - 1))
    column = jnp.exp(jax.random.uniform(key_scale, (D,), jnp.float32, math.log(0.5), math.log(2.0)))
    return (values * column[None, :] * rising[None, :] / math.sqrt(CIN)).astype(jnp.bfloat16)


def projection_values(key, columns, head_width, ramped):
    key_base, key_scale = jax.random.split(key)
    values, ramp_base = base_values(key_base, D, columns)
    column_ids = jnp.arange(columns)
    head_ids = (column_ids // head_width).astype(jnp.float32)
    rising = jnp.where(ramped(column_ids), ramp_base ** (head_ids / (HEADS - 1)), 1.0)
    column = jnp.exp(jax.random.uniform(key_scale, (columns,), jnp.float32, math.log(0.5), math.log(2.0)))
    return (values * column[None, :] * rising[None, :] / math.sqrt(D)).astype(jnp.bfloat16)


def draw_w_query(key, part):
    return projection_values(jax.random.fold_in(key, 29), HEADS * HD, HD, lambda column_ids: column_ids >= 0)


def draw_w_keyvalue(key, part):
    return projection_values(jax.random.fold_in(key, 37), HEADS * 2 * HD, 2 * HD, lambda column_ids: column_ids // HD % 2 == 0)


def shard_levels(own_key, dims, shards, low, top_value):
    def one(dim, blocks):
        steps = jax.random.uniform(jax.random.fold_in(jax.random.fold_in(own_key, 6), dim), (blocks,), jnp.float32, low / len(shards), top_value / len(shards))
        return jnp.repeat(jnp.exp(steps), dims[dim] // blocks).reshape((-1,) + (1,) * (len(dims) - dim - 1))

    loudness = one(*shards[0])
    for cut in shards[1:]:
        loudness = loudness * one(*cut)
    return loudness


def normal_values(own_key, dims, scale, limit, pieces=(), kind=jnp.bfloat16):
    drawn = scale * jax.random.normal(own_key, dims, jnp.float32)
    if pieces:
        drawn = drawn * shard_levels(own_key, dims, pieces, -0.22, 0.18)
    return jnp.clip(drawn, -limit, limit).astype(kind)


def setup_inputs(seed: int = 0) -> dict:
    seeds = jax.random.split(jax.random.key(seed), 13)
    patches = normal_values(seeds[0], (SLOTS, CIN), 1.0, 6.0, ((0, 128),))
    clip_shape = draw_clip_shape(jax.random.fold_in(seeds[12], 71), 0)
    shard_counts = draw_shard_counts(jax.random.fold_in(seeds[12], 71), 0)
    patch_weight = draw_patch_weight(jax.random.fold_in(seeds[12], 71), 0)
    patch_bias = normal_values(seeds[4], (D,), 1.0, 6.0, ((0, 2),), jnp.float32)
    time_mod = normal_values(seeds[5], (CLIPS, 2, D), 0.5, 6.0, ((2, 2),), jnp.float32)
    block_mod = normal_values(seeds[6], (2, D), 0.3, 4.0, ((1, 2),), jnp.float32)
    w_query = draw_w_query(jax.random.fold_in(seeds[12], 71), 0)
    query_bias = normal_values(seeds[8], (HEADS * HD,), 0.3, 4.0, ((0, 2),), jnp.float32)
    w_keyvalue = draw_w_keyvalue(jax.random.fold_in(seeds[12], 71), 0)
    keyvalue_bias = normal_values(seeds[10], (HEADS * 2 * HD,), 0.5, 6.0, ((0, 2),), jnp.float32)
    norm_gain = jnp.clip(jnp.exp(math.log(2.0) - 0.6931472 * jax.random.uniform(seeds[11], (2, HEADS * HD), jnp.float32) ** shard_levels(seeds[11], (2, HEADS * HD), ((1, 2),), -0.2, 0.2)), 1.0, 2.0)
    return dict(patches=patches, clip_shape=clip_shape, shard_counts=shard_counts, patch_weight=patch_weight, patch_bias=patch_bias, time_mod=time_mod, block_mod=block_mod, w_query=w_query, query_bias=query_bias, w_keyvalue=w_keyvalue, keyvalue_bias=keyvalue_bias, norm_gain=norm_gain)


EPSILON = 1e-06

def rounded(values):
    return lax.optimization_barrier(values.astype(jnp.bfloat16)).astype(jnp.float32)

def token_places(group_counts, member_ids, slot_ids, shape_row):
    before = (jnp.cumsum(group_counts) - group_counts).astype(jnp.int32)
    lookup = jnp.arange(GROUP, dtype=jnp.int32)[None, :] == member_ids[:, None]
    offset = lax.optimization_barrier(jnp.sum(jnp.where(lookup, before[None, :], 0), axis=1)).astype(jnp.int32)
    holding = lax.optimization_barrier(jnp.sum(jnp.where(lookup, group_counts[None, :], 0), axis=1)).astype(jnp.int32)
    position = offset + slot_ids
    plane_size = shape_row[1] * shape_row[2]
    frame_pos = position // plane_size
    row_pos = position // shape_row[2] % shape_row[1]
    col_pos = position % shape_row[2]
    return (slot_ids < holding, frame_pos, row_pos, col_pos)

def rotary_tables(frame_pos, row_pos, col_pos):
    other_pairs = HD // 6
    frame_pairs = HD // 2 - 2 * other_pairs
    pair_id = jnp.arange(HD, dtype=jnp.int32) // 2
    in_frame = pair_id < frame_pairs
    in_row = jnp.logical_and(pair_id >= frame_pairs, pair_id < frame_pairs + other_pairs)
    within = jnp.where(in_frame, pair_id, jnp.where(in_row, pair_id - frame_pairs, pair_id - frame_pairs - other_pairs)).astype(jnp.float32)
    axis_span = jnp.where(in_frame, 2.0 * frame_pairs, 2.0 * other_pairs).astype(jnp.float32)
    inverse = jnp.exp(-(2.0 * within / axis_span) * math.log(10000.0))
    position = jnp.where(in_frame[None, :], frame_pos[:, None], jnp.where(in_row[None, :], row_pos[:, None], col_pos[:, None])).astype(jnp.float32)
    angles = position * inverse[None, :]
    return (jnp.cos(angles), jnp.sin(angles))

def rotate_pairs(values, cosine_table, sine_table):
    parity = jnp.arange(HD, dtype=jnp.int32) % 2 == 0
    partner = jnp.where(parity, -jnp.roll(values, -1, axis=-1), jnp.roll(values, 1, axis=-1))
    return values * cosine_table[:, None, :] + partner * sine_table[:, None, :]

def modulate_rows(embedded, row_sums, squares, modulation):
    average = row_sums / D
    variance = squares / D - average * average
    normed = (embedded - average[:, None]) * lax.rsqrt(variance[:, None] + EPSILON)
    return (normed * (1.0 + modulation[1]) + modulation[0]).astype(jnp.bfloat16)

def finish_heads(raw_rows, squares, scale_gain, cosine_table, sine_table):
    normed = raw_rows * lax.rsqrt(squares[:, None] / (HEADS * HD) + EPSILON) * scale_gain
    return rotate_pairs(normed.reshape(raw_rows.shape[0], -1, HD), cosine_table, sine_table).astype(jnp.bfloat16)

def reference(patches, clip_shape, shard_counts, patch_weight, patch_bias, time_mod, block_mod, w_query, query_bias, w_keyvalue, keyvalue_bias, norm_gain):
    span_rows = GROUP * TOK_DEV
    highest = lax.Precision.HIGHEST

    def one_clip(clip_id):
        row_block = lax.dynamic_slice_in_dim(patches, (clip_id * span_rows).astype(jnp.int32), span_rows, 0)
        group_counts = lax.dynamic_slice_in_dim(shard_counts, (clip_id * GROUP).astype(jnp.int32), GROUP, 0)
        shape_row = lax.dynamic_index_in_dim(clip_shape, clip_id, 0, keepdims=False)
        slot_all = jnp.arange(span_rows, dtype=jnp.int32)
        is_valid, frame_pos, row_pos, col_pos = token_places(group_counts, slot_all // TOK_DEV, slot_all % TOK_DEV, shape_row)
        modulation = lax.dynamic_index_in_dim(time_mod, clip_id, 0, keepdims=False) + block_mod
        embedded = jnp.dot(row_block, patch_weight, preferred_element_type=jnp.float32) + patch_bias
        hidden = modulate_rows(embedded, lax.optimization_barrier(jnp.sum(embedded, axis=1)), lax.optimization_barrier(jnp.sum(embedded * embedded, axis=1)), modulation)
        query_raw = jnp.dot(hidden, w_query, preferred_element_type=jnp.float32) + query_bias
        pair_raw = (jnp.dot(hidden, w_keyvalue, preferred_element_type=jnp.float32) + keyvalue_bias).reshape(span_rows, HEADS, 2, HD)
        key_raw = pair_raw[:, :, 0].reshape(span_rows, HEADS * HD)
        value_rows = rounded(pair_raw[:, :, 1])
        cosine_table, sine_table = rotary_tables(frame_pos, row_pos, col_pos)
        queries = finish_heads(query_raw, lax.optimization_barrier(jnp.sum(query_raw * query_raw, axis=1)), norm_gain[0], cosine_table, sine_table)
        key_rows = finish_heads(key_raw, lax.optimization_barrier(jnp.sum(key_raw * key_raw, axis=1)), norm_gain[1], cosine_table, sine_table)
        queries = lax.optimization_barrier(queries).astype(jnp.float32)
        key_rows = lax.optimization_barrier(key_rows).astype(jnp.float32)
        scores = jnp.einsum('qhd,khd->hqk', queries, key_rows, precision=highest) * HD ** (-0.5)
        weights = jnp.where(is_valid[None, None, :], jnp.exp(scores), 0.0)
        totals = lax.optimization_barrier(jnp.sum(weights, axis=-1))
        numerator = jnp.einsum('hqk,khd->qhd', rounded(weights), value_rows, precision=highest)
        result = numerator / jnp.transpose(totals)[:, :, None]
        result = jnp.where(is_valid[:, None, None], result, 0.0)
        return result.reshape(span_rows, HEADS * HD).astype(jnp.bfloat16)
    outputs = lax.map(one_clip, jnp.arange(CLIPS, dtype=jnp.int32))
    return outputs.reshape(SLOTS, HEADS * HD)
```

```python
import functools
import math

import jax
import jax.numpy as jnp
from jax import lax
from jax.experimental import pallas as pl
from jax.experimental.pallas import tpu as pltpu
from jax.sharding import PartitionSpec as P

D = 2560
HALF = D // 2
HEADS = 20
HD = 128
CIN = 64
TOK = 256
PLANE = 32
COLS = 16
ROWS = 4
UNITS = 30
OWN = 5
BLOCK = 80
EPSILON = 1e-06
F32 = jnp.float32
BF16 = jnp.bfloat16
MESH = pl.DeviceIdType.MESH
HIGHEST = lax.Precision.HIGHEST


def unit_target(unit):
    is_query = unit < HEADS // 2
    pair = unit - HEADS // 2
    head = jnp.where(is_query, unit, pair // 2)
    core = head // OWN
    slot = head % OWN + jnp.where(is_query, 0, OWN + OWN * (pair % 2))
    return core, slot


def kernel(
    shape_ref,
    counts_ref,
    patches_ref,
    weight_ref,
    bias_ref,
    block_ref,
    time_ref,
    query_weight_ref,
    pair_weight_ref,
    query_bias_ref,
    pair_bias_ref,
    gain_ref,
    out_ref,
    query_ref,
    pair_ref,
    tokens,
    weight_all,
    bias_own,
    bias_all,
    block_all,
    time_all,
    centred,
    modulated,
    landed,
    columns,
    sending,
    units,
    rows_aug,
    scale_rows,
    cosines,
    sines,
    query_rows,
    key_rows,
    value_rows,
    value_ones,
    query_acc,
    key_acc,
    sums_out,
    sums_in,
    result,
    result_in,
    send_a,
    recv_a,
    send_b,
    recv_b,
    send_c,
    recv_c,
    send_p,
    recv_p,
    send_s,
    recv_s,
    send_o,
    recv_o,
    local,
):
    s = lax.axis_index("seq")
    m = lax.axis_index("mp")
    xz = s // 8
    y = (s // 2) % 4
    core = s % 2
    w = xz * 2 + core
    other = 1 - core
    owner = w < UNITS

    def plane_device(index):
        return (index // 2) * 8 + y * 2 + index % 2

    def remote(src, dst, send, recv, device):
        return pltpu.make_async_remote_copy(
            src_ref=src, dst_ref=dst, send_sem=send, recv_sem=recv, device_id=device, device_id_type=MESH
        )

    units[:, BLOCK:, :] = jnp.zeros((3 * OWN, HD - BLOCK, HD), BF16)

    bias_own[...] = bias_ref[...].reshape(1, HALF)
    query_ref[...] = query_weight_ref[...].reshape(5, 4, HALF)
    pair_ref[...] = pair_weight_ref[...].reshape(5, 4, D)

    barrier = pltpu.get_barrier_semaphore()

    def greet(step, carry):
        pl.semaphore_signal(
            barrier, inc=1, device_id=(plane_device((w + step) % PLANE), m), device_id_type=MESH
        )
        return carry

    lax.fori_loop(1, PLANE, greet, 0)
    for step in range(1, ROWS):
        pl.semaphore_signal(
            barrier,
            inc=1,
            device_id=(xz * 8 + ((y + step) % ROWS) * 2 + core, m),
            device_id_type=MESH,
        )
    pl.semaphore_signal(barrier, inc=1, device_id=(s, 1 - m), device_id_type=MESH)
    pl.semaphore_signal(barrier, inc=1, device_id=(xz * 8 + y * 2 + other, 1 - m), device_id_type=MESH)
    pl.semaphore_wait(barrier, PLANE - 1 + ROWS - 1 + 2)

    sibling = (xz * 8 + y * 2 + other, m)
    partner = (s, 1 - m)
    param_copies = [
        remote(patches_ref, tokens.at[core], send_p.at[0], recv_p.at[0], sibling),
        remote(weight_ref, weight_all.at[m], send_p.at[1], recv_p.at[1], partner),
        remote(bias_own, bias_all.at[m], send_p.at[2], recv_p.at[2], partner),
        remote(block_ref, block_all.at[m], send_p.at[3], recv_p.at[3], partner),
        remote(time_ref.at[:, y], time_all.at[m], send_p.at[4], recv_p.at[4], partner),
    ]
    own_copies = [
        pltpu.make_async_copy(patches_ref, tokens.at[core], local.at[0]),
        pltpu.make_async_copy(weight_ref, weight_all.at[m], local.at[1]),
        pltpu.make_async_copy(bias_own, bias_all.at[m], local.at[2]),
        pltpu.make_async_copy(block_ref, block_all.at[m], local.at[3]),
        pltpu.make_async_copy(time_ref.at[:, y], time_all.at[m], local.at[4]),
    ]
    for copy in param_copies + own_copies:
        copy.start()

    def query_source(unit):
        return query_ref.at[:, :, pl.ds(pl.multiple_of(unit * HD, HD), HD)]

    def pair_source(unit):
        return pair_ref.at[:, :, pl.ds(pl.multiple_of((unit - HEADS // 2) * HD, HD), HD)]

    landing = landed.at[xz, y, pl.ds(core * 5, 5)]

    def scatter(step, carry):
        unit = (w + step) % PLANE

        @pl.when(unit < HEADS // 2)
        def _():
            remote(
                query_source(unit), landing, send_a.at[step], recv_a.at[w], (plane_device(unit), m)
            ).start()

        @pl.when(jnp.logical_and(unit >= HEADS // 2, unit < UNITS))
        def _():
            remote(
                pair_source(unit), landing, send_a.at[step], recv_a.at[w], (plane_device(unit), m)
            ).start()

        return carry

    lax.fori_loop(1, PLANE, scatter, 0)

    @pl.when(w < HEADS // 2)
    def _():
        pltpu.make_async_copy(query_source(w), landing, recv_a.at[w]).start()

    @pl.when(jnp.logical_and(w >= HEADS // 2, owner))
    def _():
        pltpu.make_async_copy(pair_source(w), landing, recv_a.at[w]).start()

    clip = s // 2
    height = shape_ref[1, clip].astype(F32)
    width = shape_ref[2, clip].astype(F32)
    lane = lax.broadcasted_iota(jnp.int32, (1, HD), 1)
    other_pairs = HD // 6
    frame_pairs = HD // 2 - 2 * other_pairs
    pair_id = lane // 2
    in_frame = pair_id < frame_pairs
    in_row = jnp.logical_and(pair_id >= frame_pairs, pair_id < frame_pairs + other_pairs)
    within = jnp.where(
        in_frame,
        pair_id,
        jnp.where(in_row, pair_id - frame_pairs, pair_id - frame_pairs - other_pairs),
    ).astype(F32)
    axis_span = jnp.where(in_frame, 2.0 * frame_pairs, 2.0 * other_pairs).astype(F32)
    inverse = jnp.exp(-(2.0 * within / axis_span) * math.log(10000.0))
    even = lane % 2 == 0
    for part in range(2):
        slot = lax.broadcasted_iota(jnp.int32, (TOK, HD), 0)
        offset = counts_ref[2 * clip] if part else 0
        position = (slot + offset).astype(F32)
        line = jnp.floor((position + 0.5) / width)
        column_pos = position - line * width
        frame_pos = jnp.floor((line + 0.5) / height)
        row_pos = line - frame_pos * height
        angles = jnp.where(in_frame, frame_pos, jnp.where(in_row, row_pos, column_pos)) * inverse
        sine = jnp.sin(angles)
        cosines[part * TOK : (part + 1) * TOK, :] = jnp.cos(angles)
        sines[part * TOK : (part + 1) * TOK, :] = jnp.where(even, -sine, sine)
        valid = slot < counts_ref[2 * clip + part]
        value_ones[part * TOK : (part + 1) * TOK, :] = jnp.where(valid, 1.0, 0.0).astype(BF16)

    for copy in own_copies:
        copy.wait()
    for copy in param_copies:
        copy.wait_recv()
    for part in range(2):
        rows_aug[part * TOK : (part + 1) * TOK, 0:CIN] = tokens[part].T
    rows_aug[:, CIN:] = jnp.where(
        lax.broadcasted_iota(jnp.int32, (2 * TOK, HD - CIN), 1) < 2, 1.0, 0.0
    ).astype(BF16)

    def statistics(step, carry):
        rows = pl.ds(pl.multiple_of(step * 128, 128), 128)
        patch = rows_aug[rows, 0:CIN]
        total = jnp.zeros((128, 1), F32)
        square = jnp.zeros((128, 1), F32)
        for half in range(2):
            embedded = jnp.dot(patch, weight_all[half], preferred_element_type=F32) + bias_all[half]
            total += jnp.sum(embedded, axis=1, keepdims=True)
            square += jnp.sum(embedded * embedded, axis=1, keepdims=True)
        average = total / D
        variance = square / D - average * average
        scale_rows[rows, :] = jnp.broadcast_to(lax.rsqrt(variance + EPSILON), (128, HD))
        return carry

    lax.fori_loop(0, 4, statistics, 0)

    row_mean = (
        jnp.sum(weight_all[0].astype(F32), axis=1, keepdims=True)
        + jnp.sum(weight_all[1].astype(F32), axis=1, keepdims=True)
    ) / D
    bias_mean = (
        jnp.sum(bias_all[0], axis=1, keepdims=True) + jnp.sum(bias_all[1], axis=1, keepdims=True)
    ) / D
    for half in range(2):
        centred[half] = weight_all[half].astype(F32) - row_mean

    def modulate(step, carry):
        rows = pl.multiple_of(step * BLOCK, 16)
        index = lax.broadcasted_iota(jnp.int32, (BLOCK - CIN, HALF), 0)
        for half in range(2):
            scale = 1.0 + time_all[half, step, 1:2, :] + block_all[half, 1:2, :]
            shift = time_all[half, step, 0:1, :] + block_all[half, 0:1, :]
            span = slice(half * HALF, (half + 1) * HALF)
            modulated[pl.ds(rows, CIN), span] = (centred[half] * scale).astype(BF16)
            bias_row = (bias_all[half] - bias_mean) * scale
            bias_low = bias_row - bias_row.astype(BF16).astype(F32)
            shift_low = shift - shift.astype(BF16).astype(F32)
            extra = jnp.where(
                index == 0,
                bias_row,
                jnp.where(
                    index == 1,
                    bias_low,
                    jnp.where(index == 2, shift, jnp.where(index == 3, shift_low, 0.0)),
                ),
            )
            modulated[pl.ds(pl.multiple_of(rows + CIN, 16), BLOCK - CIN), span] = extra.astype(BF16)
        return carry

    lax.fori_loop(0, COLS, modulate, 0)

    @pl.when(owner)
    def _():
        own_landing = pltpu.make_async_copy(landing, landing, recv_a.at[w])
        own_landing.wait()

        def arrive(step, carry):
            source = (w + step) % PLANE
            block = landed.at[source // 2, y, pl.ds((source % 2) * 5, 5)]
            remote(block, block, send_a.at[0], recv_a.at[source], (plane_device(source), m)).wait_recv()
            return carry

        lax.fori_loop(1, PLANE, arrive, 0)
        spread = []
        for step in range(1, ROWS):
            spread.append(
                remote(
                    landed.at[:, y],
                    landed.at[:, y],
                    send_b.at[step - 1],
                    recv_b.at[step - 1],
                    (xz * 8 + ((y + step) % ROWS) * 2 + core, m),
                )
            )
        for copy in spread:
            copy.start()
        for step in range(1, ROWS):
            source = (y + ROWS - step) % ROWS
            remote(
                landed.at[:, source],
                landed.at[:, source],
                send_b.at[step - 1],
                recv_b.at[step - 1],
                (xz * 8 + source * 2 + core, m),
            ).wait_recv()
        columns[...] = landed[...].reshape(D, HD)
        unit_core, unit_slot = unit_target(w)

        for chunk in range(4):
            folded = jnp.dot(
                modulated[chunk * 4 * BLOCK : (chunk + 1) * 4 * BLOCK, :],
                columns[...],
                preferred_element_type=F32,
            )
            for piece in range(4):
                target = chunk * 4 + piece
                block = folded[piece * BLOCK : (piece + 1) * BLOCK]
                extra = block[CIN:]
                bias_row = extra[0:1] + extra[1:2]
                shift_row = extra[2:3] + extra[3:4]
                index = lax.broadcasted_iota(jnp.int32, (BLOCK - CIN, HD), 0)
                tail = jnp.where(
                    index == 0,
                    bias_row,
                    jnp.where(
                        index == 1,
                        bias_row - bias_row.astype(BF16).astype(F32),
                        jnp.where(
                            index == 2,
                            shift_row,
                            jnp.where(
                                index == 3, shift_row - shift_row.astype(BF16).astype(F32), 0.0
                            ),
                        ),
                    ),
                )
                sending[target, 0:CIN, :] = block[:CIN].astype(BF16)
                sending[target, CIN:, :] = tail.astype(BF16)
                device = target * 8 + y * 2 + unit_core

                @pl.when(device != s)
                def _():
                    remote(
                        sending.at[target],
                        units.at[unit_slot, pl.ds(0, BLOCK)],
                        send_c.at[target],
                        recv_c.at[unit_slot],
                        (device, m),
                    ).start()

                @pl.when(device == s)
                def _():
                    pltpu.make_async_copy(
                        sending.at[target], units.at[unit_slot, pl.ds(0, BLOCK)], recv_c.at[unit_slot]
                    ).start()

    def collect(slot, carry):
        block = units.at[slot, pl.ds(0, BLOCK)]
        pltpu.make_async_copy(block, block, recv_c.at[slot]).wait()
        return carry

    query_acc[...] = jnp.zeros_like(query_acc)
    key_acc[...] = jnp.zeros_like(key_acc)

    def raw_rows(slot, rows, bias_row):
        unit = units[slot]
        shift_row = unit[CIN + 2 : CIN + 3].astype(F32) + unit[CIN + 3 : CIN + 4].astype(F32)
        product = jnp.dot(rows_aug[rows, :], unit, preferred_element_type=F32)
        return product * scale_rows[rows, :] + (shift_row + bias_row)

    def rotated(values, rows):
        partner_rows = jnp.where(even, pltpu.roll(values, HD - 1, 1), pltpu.roll(values, 1, 1))
        return values * cosines[rows, :] + partner_rows * sines[rows, :]

    lax.fori_loop(0, 2 * OWN, collect, 0)

    def project(head, carry):
        column = pl.multiple_of((core * OWN + head) * HD, HD)
        query_bias = query_bias_ref[pl.ds(column, HD)].reshape(1, HD)
        key_bias = pair_bias_ref[pl.ds(pl.multiple_of(column * 2, HD), HD)].reshape(1, HD)
        for part in range(2):
            rows = slice(part * TOK, (part + 1) * TOK)
            raw = raw_rows(head, rows, query_bias)
            query_acc[rows, :] += raw * raw
            query_rows[head, rows, :] = rotated(raw * gain_ref[0:1, pl.ds(column, HD)], rows)
            raw = raw_rows(OWN + head, rows, key_bias)
            key_acc[rows, :] += raw * raw
            key_rows[head, rows, :] = rotated(raw * gain_ref[1:2, pl.ds(column, HD)], rows)
        return carry

    lax.fori_loop(0, OWN, project, 0)

    ones = jnp.ones((8, HD), F32)
    contract_lanes = (((1,), (1,)), ((), ()))
    contract_rows = (((0,), (0,)), ((), ()))
    query_sums = lax.dot_general(
        ones, query_acc[...], contract_lanes, precision=HIGHEST, preferred_element_type=F32
    )
    key_sums = lax.dot_general(
        ones, key_acc[...], contract_lanes, precision=HIGHEST, preferred_element_type=F32
    )
    sum_index = lax.broadcasted_iota(jnp.int32, (8, 2 * TOK), 0)
    sums_out[...] = jnp.where(sum_index == 0, query_sums, key_sums)
    sum_copies = [
        remote(sums_out, sums_in.at[0], send_s.at[0], recv_s.at[0], sibling),
        remote(sums_out, sums_in.at[1], send_s.at[1], recv_s.at[1], partner),
        remote(
            sums_out,
            sums_in.at[2],
            send_s.at[2],
            recv_s.at[2],
            (xz * 8 + y * 2 + other, 1 - m),
        ),
    ]
    for copy in sum_copies:
        copy.start()

    def collect_value(head, carry):
        return collect(2 * OWN + head, carry)

    lax.fori_loop(0, OWN, collect_value, 0)

    def values(head, carry):
        column = pl.multiple_of(((core * OWN + head) * 2 + 1) * HD, HD)
        value_bias = pair_bias_ref[pl.ds(column, HD)].reshape(1, HD)
        for part in range(2):
            rows = slice(part * TOK, (part + 1) * TOK)
            raw = raw_rows(2 * OWN + head, rows, value_bias)
            slot = lax.broadcasted_iota(jnp.int32, (TOK, HD), 0)
            kept = jnp.where(slot < counts_ref[2 * clip + part], raw, 0.0)
            value_rows[head, rows, :] = kept.astype(BF16)
        return carry

    lax.fori_loop(0, OWN, values, 0)

    for copy in sum_copies:
        copy.wait_recv()
    square_sums = sums_out[...] + sums_in[0] + sums_in[1] + sums_in[2]
    factors = lax.rsqrt(square_sums / (HEADS * HD) + EPSILON)
    query_factor = lax.dot_general(
        jnp.where(sum_index == 0, factors * (HD**-0.5 * math.log2(math.e)), 0.0),
        ones,
        contract_rows,
        precision=HIGHEST,
        preferred_element_type=F32,
    )
    key_factor = lax.dot_general(
        jnp.where(sum_index == 1, factors, 0.0),
        ones,
        contract_rows,
        precision=HIGHEST,
        preferred_element_type=F32,
    )
    query_acc[...] = query_factor
    key_acc[...] = jnp.where(value_ones[...].astype(F32) > 0.0, key_factor, 0.0)

    def attend(head, carry):
        keys = (key_rows[head] * key_acc[...]).astype(BF16)
        for part in range(2):
            rows = slice(part * TOK, (part + 1) * TOK)
            queries = (query_rows[head, rows, :] * query_acc[rows, :]).astype(BF16)
            scores = lax.dot_general(queries, keys, contract_lanes, preferred_element_type=F32)
            weights = jnp.exp2(scores).astype(BF16)
            numerator = jnp.dot(weights, value_rows[head], preferred_element_type=F32)
            totals = jnp.dot(weights, value_ones[...], preferred_element_type=F32)
            slot = lax.broadcasted_iota(jnp.int32, (TOK, HD), 0)
            kept = jnp.where(slot < counts_ref[2 * clip + part], numerator / totals, 0.0)
            result[part, head] = kept.astype(BF16)
        remote(
            result.at[other, head], result_in.at[head], send_o.at[head], recv_o.at[head], sibling
        ).start()
        return carry

    lax.fori_loop(0, OWN, attend, 0)

    for side in range(2):
        @pl.when(core == side)
        def _():
            for head in range(OWN):
                column = (side * OWN + head) * HD
                out_ref[:, column : column + HD] = result[side, head]

    for head in range(OWN):
        remote(
            result.at[other, head], result_in.at[head], send_o.at[head], recv_o.at[head], sibling
        ).wait()

    for side in range(2):
        @pl.when(core == side)
        def _():
            for head in range(OWN):
                column = ((1 - side) * OWN + head) * HD
                out_ref[:, column : column + HD] = result_in[head]

    for copy in param_copies + sum_copies:
        copy.wait_send()

    def sent(step, carry):
        @pl.when((w + step) % PLANE < UNITS)
        def _():
            remote(query_source(0), landing, send_a.at[step], recv_a.at[w], partner).wait_send()

        return carry

    lax.fori_loop(1, PLANE, sent, 0)

    @pl.when(owner)
    def _():
        for step in range(1, ROWS):
            remote(
                landed.at[:, y], landed.at[:, y], send_b.at[step - 1], recv_b.at[step - 1], partner
            ).wait_send()
        unit_core, unit_slot = unit_target(w)

        def sent_block(target, carry):
            @pl.when(target * 8 + y * 2 + unit_core != s)
            def _():
                remote(
                    sending.at[target],
                    units.at[unit_slot, pl.ds(0, BLOCK)],
                    send_c.at[target],
                    recv_c.at[unit_slot],
                    partner,
                ).wait_send()

            return carry

        lax.fori_loop(0, COLS, sent_block, 0)


def shards(
    patches,
    clip_shape,
    shard_counts,
    patch_weight,
    patch_bias,
    time_mod,
    block_mod,
    w_query,
    query_bias,
    w_keyvalue,
    keyvalue_bias,
    norm_gain,
):
    vmem = pl.BlockSpec(memory_space=pltpu.VMEM)
    smem = pl.BlockSpec(memory_space=pltpu.SMEM)
    anywhere = pl.BlockSpec(memory_space=pl.ANY)
    dma = pltpu.SemaphoreType.DMA
    return pl.pallas_call(
        kernel,
        out_shape=jax.ShapeDtypeStruct((TOK, HALF), BF16),
        in_specs=[smem, smem, vmem, vmem, vmem, vmem, anywhere, vmem, vmem, vmem, vmem, vmem],
        out_specs=vmem,
        scratch_shapes=[
            pltpu.VMEM((5, 4, HALF), BF16),
            pltpu.VMEM((5, 4, D), BF16),
            pltpu.VMEM((2, CIN, TOK), BF16),
            pltpu.VMEM((2, CIN, HALF), BF16),
            pltpu.VMEM((1, HALF), F32),
            pltpu.VMEM((2, 1, HALF), F32),
            pltpu.VMEM((2, 2, HALF), F32),
            pltpu.VMEM((2, COLS, 2, HALF), F32),
            pltpu.VMEM((2, CIN, HALF), F32),
            pltpu.VMEM((COLS * BLOCK, D), BF16),
            pltpu.VMEM((COLS, ROWS, 10, 4, HD), BF16),
            pltpu.VMEM((D, HD), BF16),
            pltpu.VMEM((COLS, BLOCK, HD), BF16),
            pltpu.VMEM((3 * OWN, HD, HD), BF16),
            pltpu.VMEM((2 * TOK, HD), BF16),
            pltpu.VMEM((2 * TOK, HD), F32),
            pltpu.VMEM((2 * TOK, HD), F32),
            pltpu.VMEM((2 * TOK, HD), F32),
            pltpu.VMEM((OWN, 2 * TOK, HD), F32),
            pltpu.VMEM((OWN, 2 * TOK, HD), F32),
            pltpu.VMEM((OWN, 2 * TOK, HD), BF16),
            pltpu.VMEM((2 * TOK, HD), BF16),
            pltpu.VMEM((2 * TOK, HD), F32),
            pltpu.VMEM((2 * TOK, HD), F32),
            pltpu.VMEM((8, 2 * TOK), F32),
            pltpu.VMEM((3, 8, 2 * TOK), F32),
            pltpu.VMEM((2, OWN, TOK, HD), BF16),
            pltpu.VMEM((OWN, TOK, HD), BF16),
            dma((PLANE,)),
            dma((PLANE,)),
            dma((ROWS - 1,)),
            dma((ROWS - 1,)),
            dma((COLS,)),
            dma((3 * OWN,)),
            dma((5,)),
            dma((5,)),
            dma((3,)),
            dma((3,)),
            dma((OWN,)),
            dma((OWN,)),
            dma((5,)),
        ],
        compiler_params=pltpu.CompilerParams(
            collective_id=0, has_side_effects=True, vmem_limit_bytes=60 << 20
        ),
    )(
        clip_shape.T,
        shard_counts,
        patches.T,
        patch_weight,
        patch_bias,
        block_mod,
        time_mod.reshape(COLS, ROWS, 2, HALF),
        w_query,
        w_keyvalue,
        query_bias,
        keyvalue_bias,
        norm_gain,
    )


def solution(mesh):
    return jax.shard_map(
        shards,
        mesh=mesh,
        in_specs=(
            P("seq", None),
            P(),
            P(),
            P(None, "mp"),
            P("mp"),
            P(None, None, "mp"),
            P(None, "mp"),
            P("seq", "mp"),
            P("mp"),
            P("seq", "mp"),
            P("mp"),
            P(None, "mp"),
        ),
        out_specs=P("seq", "mp"),
        check_vma=False,
    )
```

```python
import functools
import math

import jax
import jax.numpy as jnp
from jax import lax
from jax.experimental import pallas as pl
from jax.experimental.pallas import tpu as pltpu
from jax.sharding import PartitionSpec as P

D = 2560
HALF = D // 2
HEADS = 20
HD = 128
CIN = 64
TOK = 256
PLANE = 32
CLIPS_HERE = 16
UNITS = 30
OWN = 5
BLOCK = 80
EPSILON = 1e-06
F32 = jnp.float32
BF16 = jnp.bfloat16
MESH = pl.DeviceIdType.MESH
HIGHEST = lax.Precision.HIGHEST


def unit_target(unit):
    is_query = unit < HEADS // 2
    pair = unit - HEADS // 2
    head = jnp.where(is_query, unit, pair // 2)
    core = head // OWN
    slot = head % OWN + jnp.where(is_query, 0, OWN + OWN * (pair % 2))
    return core, slot


def kernel(
    shape_ref,
    counts_ref,
    patches_ref,
    weight_ref,
    bias_ref,
    block_ref,
    time_ref,
    query_weight_ref,
    pair_weight_ref,
    query_bias_ref,
    pair_bias_ref,
    gain_ref,
    out_ref,
    query_ref,
    pair_ref,
    tokens,
    weight_all,
    bias_own,
    bias_all,
    block_all,
    time_all,
    centred,
    modulated,
    landed,
    columns,
    sending,
    units,
    rows_aug,
    scale_rows,
    cosines,
    sines,
    query_rows,
    key_rows,
    value_rows,
    value_ones,
    query_acc,
    key_acc,
    sums_out,
    sums_in,
    result,
    result_in,
    send_a,
    recv_a,
    send_b,
    recv_b,
    send_c,
    recv_c,
    send_p,
    recv_p,
    send_s,
    recv_s,
    send_o,
    recv_o,
    local,
):
    s = lax.axis_index("seq")
    m = lax.axis_index("mp")
    x_lo = s // (2 * PLANE)
    chip = (s // 2) % PLANE
    core = s % 2
    other = 1 - core
    owner = chip < UNITS
    unit_core, unit_slot = unit_target(chip)
    crossing = jnp.logical_and(owner, unit_core != core)

    def plane_device(index, side):
        return (x_lo * 2 * PLANE + index * 2 + side, m)

    sibling = plane_device(chip, other)
    partner = (s, 1 - m)
    diagonal = (sibling[0], 1 - m)
    neighbour = (s + 2 * PLANE * (1 - 2 * x_lo), m)

    def remote(src, dst, send, recv, device):
        return pltpu.make_async_remote_copy(
            src_ref=src, dst_ref=dst, send_sem=send, recv_sem=recv, device_id=device, device_id_type=MESH
        )

    units[:, BLOCK:, :] = jnp.zeros((3 * OWN, HD - BLOCK, HD), BF16)

    bias_own[...] = bias_ref[...].reshape(1, HALF)
    query_ref[...] = query_weight_ref[...].reshape(5, 4, HALF)
    pair_ref[...] = pair_weight_ref[...].reshape(5, 4, D)

    barrier = pltpu.get_barrier_semaphore()

    def greet(step, carry):
        pl.semaphore_signal(
            barrier, inc=1, device_id=plane_device((chip + step) % PLANE, core), device_id_type=MESH
        )
        return carry

    lax.fori_loop(1, PLANE, greet, 0)
    for device in (sibling, partner, diagonal, neighbour):
        pl.semaphore_signal(barrier, inc=1, device_id=device, device_id_type=MESH)

    @pl.when(chip // CLIPS_HERE != core)
    def _():
        def greet_owner(step, carry):
            unit = jnp.where(
                step < OWN, core * OWN + step, HEADS // 2 + core * 2 * OWN + step - OWN
            )
            pl.semaphore_signal(
                barrier, inc=1, device_id=plane_device(unit, other), device_id_type=MESH
            )
            return carry

        lax.fori_loop(0, 3 * OWN, greet_owner, 0)

    pl.semaphore_wait(barrier, PLANE - 1 + 4 + jnp.where(crossing, CLIPS_HERE, 0))

    half_rows = pl.ds(pl.multiple_of(core * (CIN // 2), CIN // 2), CIN // 2)
    own_clips = pl.ds(x_lo * PLANE + core * CLIPS_HERE, CLIPS_HERE)
    param_copies = [
        remote(patches_ref, tokens.at[core], send_p.at[0], recv_p.at[0], sibling),
        remote(weight_ref.at[half_rows], weight_all.at[m, core], send_p.at[1], recv_p.at[1], partner),
        remote(bias_own, bias_all.at[m], send_p.at[2], recv_p.at[2], partner),
        remote(block_ref, block_all.at[m], send_p.at[3], recv_p.at[3], partner),
        remote(time_ref.at[own_clips], time_all.at[m], send_p.at[4], recv_p.at[4], partner),
    ]
    own_copies = [
        pltpu.make_async_copy(patches_ref, tokens.at[core], local.at[0]),
        pltpu.make_async_copy(weight_ref.at[pl.ds(0, CIN // 2)], weight_all.at[m, 0], local.at[1]),
        pltpu.make_async_copy(weight_ref.at[pl.ds(CIN // 2, CIN // 2)], weight_all.at[m, 1], local.at[5]),
        pltpu.make_async_copy(bias_own, bias_all.at[m], local.at[2]),
        pltpu.make_async_copy(block_ref, block_all.at[m], local.at[3]),
        pltpu.make_async_copy(time_ref.at[own_clips], time_all.at[m], local.at[4]),
    ]
    for copy in param_copies + own_copies:
        copy.start()

    def query_source(unit):
        return query_ref.at[:, :, pl.ds(pl.multiple_of(unit * HD, HD), HD)]

    def pair_source(unit):
        return pair_ref.at[:, :, pl.ds(pl.multiple_of((unit - HEADS // 2) * HD, HD), HD)]

    landing = landed.at[x_lo, chip, core]

    def scatter(step, carry):
        unit = (chip + step) % PLANE

        @pl.when(unit < HEADS // 2)
        def _():
            remote(
                query_source(unit), landing, send_a.at[step], recv_a.at[chip], plane_device(unit, core)
            ).start()

        @pl.when(jnp.logical_and(unit >= HEADS // 2, unit < UNITS))
        def _():
            remote(
                pair_source(unit), landing, send_a.at[step], recv_a.at[chip], plane_device(unit, core)
            ).start()

        return carry

    lax.fori_loop(1, PLANE, scatter, 0)

    @pl.when(chip < HEADS // 2)
    def _():
        pltpu.make_async_copy(query_source(chip), landing, recv_a.at[chip]).start()

    @pl.when(jnp.logical_and(chip >= HEADS // 2, owner))
    def _():
        pltpu.make_async_copy(pair_source(chip), landing, recv_a.at[chip]).start()

    clip = s // 2
    height = shape_ref[1, clip].astype(F32)
    width = shape_ref[2, clip].astype(F32)
    lane = lax.broadcasted_iota(jnp.int32, (1, HD), 1)
    other_pairs = HD // 6
    frame_pairs = HD // 2 - 2 * other_pairs
    pair_id = lane // 2
    in_frame = pair_id < frame_pairs
    in_row = jnp.logical_and(pair_id >= frame_pairs, pair_id < frame_pairs + other_pairs)
    within = jnp.where(
        in_frame,
        pair_id,
        jnp.where(in_row, pair_id - frame_pairs, pair_id - frame_pairs - other_pairs),
    ).astype(F32)
    axis_span = jnp.where(in_frame, 2.0 * frame_pairs, 2.0 * other_pairs).astype(F32)
    inverse = jnp.exp(-(2.0 * within / axis_span) * math.log(10000.0))
    even = lane % 2 == 0
    for part in range(2):
        slot = lax.broadcasted_iota(jnp.int32, (TOK, HD), 0)
        offset = counts_ref[2 * clip] if part else 0
        position = (slot + offset).astype(F32)
        line = jnp.floor((position + 0.5) / width)
        column_pos = position - line * width
        frame_pos = jnp.floor((line + 0.5) / height)
        row_pos = line - frame_pos * height
        angles = jnp.where(in_frame, frame_pos, jnp.where(in_row, row_pos, column_pos)) * inverse
        sine = jnp.sin(angles)
        cosines[part * TOK : (part + 1) * TOK, :] = jnp.cos(angles)
        sines[part * TOK : (part + 1) * TOK, :] = jnp.where(even, -sine, sine)
        valid = slot < counts_ref[2 * clip + part]
        value_ones[part * TOK : (part + 1) * TOK, :] = jnp.where(valid, 1.0, 0.0).astype(BF16)

    here = landed.at[x_lo, :, core]
    there = landed.at[1 - x_lo, :, core]
    to_sibling = remote(here, here, send_b.at[0], recv_b.at[0], sibling)
    to_neighbour = remote(here, here, send_b.at[1], recv_b.at[1], neighbour)
    passed_on = remote(there, there, send_b.at[2], recv_b.at[2], sibling)

    @pl.when(owner)
    def _():
        pltpu.make_async_copy(landing, landing, recv_a.at[chip]).wait()

        def arrive(step, carry):
            source = (chip + step) % PLANE
            block = landed.at[x_lo, source, core]
            remote(
                block, block, send_a.at[0], recv_a.at[source], plane_device(source, core)
            ).wait_recv()
            return carry

        lax.fori_loop(1, PLANE, arrive, 0)
        to_neighbour.start()
        to_sibling.start()

    param_copies[1].wait_recv()
    weight_block = weight_all.at[1 - m, core]
    shared = remote(weight_block, weight_block, send_p.at[5], recv_p.at[5], sibling)
    shared.start()
    for copy in own_copies:
        copy.wait()
    for copy in param_copies[:1] + param_copies[2:] + [shared]:
        copy.wait_recv()
    for part in range(2):
        rows_aug[part * TOK : (part + 1) * TOK, 0:CIN] = tokens[part].T
    rows_aug[:, CIN:] = jnp.where(
        lax.broadcasted_iota(jnp.int32, (2 * TOK, HD - CIN), 1) < 2, 1.0, 0.0
    ).astype(BF16)

    def statistics(step, carry):
        rows = pl.ds(pl.multiple_of(step * 128, 128), 128)
        patch = rows_aug[rows, 0:CIN]
        total = jnp.zeros((128, 1), F32)
        square = jnp.zeros((128, 1), F32)
        for half in range(2):
            embedded = jnp.dot(patch, weight_all[half].reshape(CIN, HALF), preferred_element_type=F32) + bias_all[half]
            total += jnp.sum(embedded, axis=1, keepdims=True)
            square += jnp.sum(embedded * embedded, axis=1, keepdims=True)
        average = total / D
        variance = square / D - average * average
        scale_rows[rows, :] = jnp.broadcast_to(lax.rsqrt(variance + EPSILON), (128, HD))
        return carry

    lax.fori_loop(0, 4, statistics, 0)

    row_mean = (
        jnp.sum(weight_all[0].reshape(CIN, HALF).astype(F32), axis=1, keepdims=True)
        + jnp.sum(weight_all[1].reshape(CIN, HALF).astype(F32), axis=1, keepdims=True)
    ) / D
    bias_mean = (
        jnp.sum(bias_all[0], axis=1, keepdims=True) + jnp.sum(bias_all[1], axis=1, keepdims=True)
    ) / D
    for half in range(2):
        centred[half] = weight_all[half].reshape(CIN, HALF).astype(F32) - row_mean

    def modulate(step, carry):
        rows = pl.multiple_of(step * BLOCK, 16)
        index = lax.broadcasted_iota(jnp.int32, (BLOCK - CIN, HALF), 0)
        for half in range(2):
            scale = 1.0 + time_all[half, step, 1:2, :] + block_all[half, 1:2, :]
            shift = time_all[half, step, 0:1, :] + block_all[half, 0:1, :]
            span = slice(half * HALF, (half + 1) * HALF)
            modulated[pl.ds(rows, CIN), span] = (centred[half] * scale).astype(BF16)
            bias_row = (bias_all[half] - bias_mean) * scale
            bias_low = bias_row - bias_row.astype(BF16).astype(F32)
            shift_low = shift - shift.astype(BF16).astype(F32)
            extra = jnp.where(
                index == 0,
                bias_row,
                jnp.where(
                    index == 1,
                    bias_low,
                    jnp.where(index == 2, shift, jnp.where(index == 3, shift_low, 0.0)),
                ),
            )
            modulated[pl.ds(pl.multiple_of(rows + CIN, 16), BLOCK - CIN), span] = extra.astype(BF16)
        return carry

    lax.fori_loop(0, CLIPS_HERE, modulate, 0)

    @pl.when(owner)
    def _():
        to_neighbour.wait_recv()
        passed_on.start()
        to_sibling.wait_recv()
        passed_on.wait_recv()
        columns[...] = landed[...].reshape(D, HD)

        for turn in range(4):
            chunk = (turn + chip) % 4
            folded = jnp.dot(
                modulated[pl.ds(pl.multiple_of(chunk * 4 * BLOCK, 4 * BLOCK), 4 * BLOCK), :],
                columns[...],
                preferred_element_type=F32,
            )
            for piece in range(4):
                target = chunk * 4 + piece
                block = folded[piece * BLOCK : (piece + 1) * BLOCK]
                extra = block[CIN:]
                bias_row = extra[0:1] + extra[1:2]
                shift_row = extra[2:3] + extra[3:4]
                index = lax.broadcasted_iota(jnp.int32, (BLOCK - CIN, HD), 0)
                tail = jnp.where(
                    index == 0,
                    bias_row,
                    jnp.where(
                        index == 1,
                        bias_row - bias_row.astype(BF16).astype(F32),
                        jnp.where(
                            index == 2,
                            shift_row,
                            jnp.where(
                                index == 3, shift_row - shift_row.astype(BF16).astype(F32), 0.0
                            ),
                        ),
                    ),
                )
                sending[target, 0:CIN, :] = block[:CIN].astype(BF16)
                sending[target, CIN:, :] = tail.astype(BF16)

            for piece in range(4):
                target = chunk * 4 + (piece + chip // 4) % 4
                device = plane_device(core * CLIPS_HERE + target, unit_core)

                @pl.when(device[0] != s)
                def _():
                    remote(
                        sending.at[target],
                        units.at[unit_slot, pl.ds(0, BLOCK)],
                        send_c.at[target],
                        recv_c.at[unit_slot],
                        device,
                    ).start()

                @pl.when(device[0] == s)
                def _():
                    pltpu.make_async_copy(
                        sending.at[target], units.at[unit_slot, pl.ds(0, BLOCK)], recv_c.at[unit_slot]
                    ).start()

    def collect(slot, carry):
        block = units.at[slot, pl.ds(0, BLOCK)]
        pltpu.make_async_copy(block, block, recv_c.at[slot]).wait()
        return carry

    query_acc[...] = jnp.zeros_like(query_acc)
    key_acc[...] = jnp.zeros_like(key_acc)

    def raw_rows(slot, rows, bias_row):
        unit = units[slot]
        shift_row = unit[CIN + 2 : CIN + 3].astype(F32) + unit[CIN + 3 : CIN + 4].astype(F32)
        product = jnp.dot(rows_aug[rows, :], unit, preferred_element_type=F32)
        return product * scale_rows[rows, :] + (shift_row + bias_row)

    def rotated(values, rows):
        partner_rows = jnp.where(even, pltpu.roll(values, HD - 1, 1), pltpu.roll(values, 1, 1))
        return values * cosines[rows, :] + partner_rows * sines[rows, :]

    lax.fori_loop(0, 2 * OWN, collect, 0)

    def project(head, carry):
        column = pl.multiple_of((core * OWN + head) * HD, HD)
        query_bias = query_bias_ref[pl.ds(column, HD)].reshape(1, HD)
        key_bias = pair_bias_ref[pl.ds(pl.multiple_of(column * 2, HD), HD)].reshape(1, HD)
        for part in range(2):
            rows = slice(part * TOK, (part + 1) * TOK)
            raw = raw_rows(head, rows, query_bias)
            query_acc[rows, :] += raw * raw
            query_rows[head, rows, :] = rotated(raw * gain_ref[0:1, pl.ds(column, HD)], rows)
            raw = raw_rows(OWN + head, rows, key_bias)
            key_acc[rows, :] += raw * raw
            key_rows[head, rows, :] = rotated(raw * gain_ref[1:2, pl.ds(column, HD)], rows)
        return carry

    lax.fori_loop(0, OWN, project, 0)

    ones = jnp.ones((8, HD), F32)
    contract_lanes = (((1,), (1,)), ((), ()))
    contract_rows = (((0,), (0,)), ((), ()))
    query_sums = lax.dot_general(
        ones, query_acc[...], contract_lanes, precision=HIGHEST, preferred_element_type=F32
    )
    key_sums = lax.dot_general(
        ones, key_acc[...], contract_lanes, precision=HIGHEST, preferred_element_type=F32
    )
    sum_index = lax.broadcasted_iota(jnp.int32, (8, 2 * TOK), 0)
    sums_out[...] = jnp.where(sum_index == 0, query_sums, key_sums)
    sum_copies = [
        remote(sums_out, sums_in.at[0], send_s.at[0], recv_s.at[0], sibling),
        remote(sums_out, sums_in.at[1], send_s.at[1], recv_s.at[1], partner),
        remote(
            sums_out,
            sums_in.at[2],
            send_s.at[2],
            recv_s.at[2],
            diagonal,
        ),
    ]
    for copy in sum_copies:
        copy.start()

    def collect_value(head, carry):
        return collect(2 * OWN + head, carry)

    lax.fori_loop(0, OWN, collect_value, 0)

    def values(head, carry):
        column = pl.multiple_of(((core * OWN + head) * 2 + 1) * HD, HD)
        value_bias = pair_bias_ref[pl.ds(column, HD)].reshape(1, HD)
        for part in range(2):
            rows = slice(part * TOK, (part + 1) * TOK)
            raw = raw_rows(2 * OWN + head, rows, value_bias)
            slot = lax.broadcasted_iota(jnp.int32, (TOK, HD), 0)
            kept = jnp.where(slot < counts_ref[2 * clip + part], raw, 0.0)
            value_rows[head, rows, :] = kept.astype(BF16)
        return carry

    lax.fori_loop(0, OWN, values, 0)

    for copy in sum_copies:
        copy.wait_recv()
    square_sums = sums_out[...] + sums_in[0] + sums_in[1] + sums_in[2]
    factors = lax.rsqrt(square_sums / (HEADS * HD) + EPSILON)
    query_factor = lax.dot_general(
        jnp.where(sum_index == 0, factors * (HD**-0.5 * math.log2(math.e)), 0.0),
        ones,
        contract_rows,
        precision=HIGHEST,
        preferred_element_type=F32,
    )
    key_factor = lax.dot_general(
        jnp.where(sum_index == 1, factors, 0.0),
        ones,
        contract_rows,
        precision=HIGHEST,
        preferred_element_type=F32,
    )
    query_acc[...] = query_factor
    key_acc[...] = jnp.where(value_ones[...].astype(F32) > 0.0, key_factor, 0.0)

    def attend(head, carry):
        keys = (key_rows[head] * key_acc[...]).astype(BF16)
        for part in range(2):
            rows = slice(part * TOK, (part + 1) * TOK)
            queries = (query_rows[head, rows, :] * query_acc[rows, :]).astype(BF16)
            scores = lax.dot_general(queries, keys, contract_lanes, preferred_element_type=F32)
            weights = jnp.exp2(scores).astype(BF16)
            numerator = jnp.dot(weights, value_rows[head], preferred_element_type=F32)
            totals = jnp.dot(weights, value_ones[...], preferred_element_type=F32)
            slot = lax.broadcasted_iota(jnp.int32, (TOK, HD), 0)
            kept = jnp.where(slot < counts_ref[2 * clip + part], numerator / totals, 0.0)
            result[part, head] = kept.astype(BF16)
        remote(
            result.at[other, head], result_in.at[head], send_o.at[head], recv_o.at[head], sibling
        ).start()
        return carry

    lax.fori_loop(0, OWN, attend, 0)

    for side in range(2):
        @pl.when(core == side)
        def _():
            for head in range(OWN):
                column = (side * OWN + head) * HD
                out_ref[:, column : column + HD] = result[side, head]

    for head in range(OWN):
        remote(
            result.at[other, head], result_in.at[head], send_o.at[head], recv_o.at[head], sibling
        ).wait()

    for side in range(2):
        @pl.when(core == side)
        def _():
            for head in range(OWN):
                column = ((1 - side) * OWN + head) * HD
                out_ref[:, column : column + HD] = result_in[head]

    for copy in param_copies + [shared] + sum_copies:
        copy.wait_send()

    def sent(step, carry):
        @pl.when((chip + step) % PLANE < UNITS)
        def _():
            remote(query_source(0), landing, send_a.at[step], recv_a.at[chip], partner).wait_send()

        return carry

    lax.fori_loop(1, PLANE, sent, 0)

    @pl.when(owner)
    def _():
        for copy in (to_sibling, to_neighbour, passed_on):
            copy.wait_send()

        def sent_block(target, carry):
            @pl.when(plane_device(core * CLIPS_HERE + target, unit_core)[0] != s)
            def _():
                remote(
                    sending.at[target],
                    units.at[unit_slot, pl.ds(0, BLOCK)],
                    send_c.at[target],
                    recv_c.at[unit_slot],
                    partner,
                ).wait_send()

            return carry

        lax.fori_loop(0, CLIPS_HERE, sent_block, 0)


def shards(
    patches,
    clip_shape,
    shard_counts,
    patch_weight,
    patch_bias,
    time_mod,
    block_mod,
    w_query,
    query_bias,
    w_keyvalue,
    keyvalue_bias,
    norm_gain,
):
    vmem = pl.BlockSpec(memory_space=pltpu.VMEM)
    smem = pl.BlockSpec(memory_space=pltpu.SMEM)
    anywhere = pl.BlockSpec(memory_space=pl.ANY)
    dma = pltpu.SemaphoreType.DMA
    return pl.pallas_call(
        kernel,
        out_shape=jax.ShapeDtypeStruct((TOK, HALF), BF16),
        in_specs=[smem, smem, vmem, vmem, vmem, vmem, anywhere, vmem, vmem, vmem, vmem, vmem],
        out_specs=vmem,
        scratch_shapes=[
            pltpu.VMEM((5, 4, HALF), BF16),
            pltpu.VMEM((5, 4, D), BF16),
            pltpu.VMEM((2, CIN, TOK), BF16),
            pltpu.VMEM((2, 2, CIN // 2, HALF), BF16),
            pltpu.VMEM((1, HALF), F32),
            pltpu.VMEM((2, 1, HALF), F32),
            pltpu.VMEM((2, 2, HALF), F32),
            pltpu.VMEM((2, CLIPS_HERE, 2, HALF), F32),
            pltpu.VMEM((2, CIN, HALF), F32),
            pltpu.VMEM((CLIPS_HERE * BLOCK, D), BF16),
            pltpu.VMEM((2, PLANE, 2, 5, 4, HD), BF16),
            pltpu.VMEM((D, HD), BF16),
            pltpu.VMEM((CLIPS_HERE, BLOCK, HD), BF16),
            pltpu.VMEM((3 * OWN, HD, HD), BF16),
            pltpu.VMEM((2 * TOK, HD), BF16),
            pltpu.VMEM((2 * TOK, HD), F32),
            pltpu.VMEM((2 * TOK, HD), F32),
            pltpu.VMEM((2 * TOK, HD), F32),
            pltpu.VMEM((OWN, 2 * TOK, HD), F32),
            pltpu.VMEM((OWN, 2 * TOK, HD), F32),
            pltpu.VMEM((OWN, 2 * TOK, HD), BF16),
            pltpu.VMEM((2 * TOK, HD), BF16),
            pltpu.VMEM((2 * TOK, HD), F32),
            pltpu.VMEM((2 * TOK, HD), F32),
            pltpu.VMEM((8, 2 * TOK), F32),
            pltpu.VMEM((3, 8, 2 * TOK), F32),
            pltpu.VMEM((2, OWN, TOK, HD), BF16),
            pltpu.VMEM((OWN, TOK, HD), BF16),
            dma((PLANE,)),
            dma((PLANE,)),
            dma((3,)),
            dma((3,)),
            dma((CLIPS_HERE,)),
            dma((3 * OWN,)),
            dma((6,)),
            dma((6,)),
            dma((3,)),
            dma((3,)),
            dma((OWN,)),
            dma((OWN,)),
            dma((6,)),
        ],
        compiler_params=pltpu.CompilerParams(
            collective_id=0, has_side_effects=True, vmem_limit_bytes=60 << 20
        ),
    )(
        clip_shape.T,
        shard_counts,
        patches.T,
        patch_weight,
        patch_bias,
        block_mod,
        time_mod,
        w_query,
        w_keyvalue,
        query_bias,
        keyvalue_bias,
        norm_gain,
    )


def solution(mesh):
    return jax.shard_map(
        shards,
        mesh=mesh,
        in_specs=(
            P("seq", None),
            P(),
            P(),
            P(None, "mp"),
            P("mp"),
            P(None, None, "mp"),
            P(None, "mp"),
            P("seq", "mp"),
            P("mp"),
            P("seq", "mp"),
            P("mp"),
            P(None, "mp"),
        ),
        out_specs=P("seq", "mp"),
        check_vma=False,
    )
```

```python
import functools
import math

import jax
import jax.numpy as jnp
from jax import lax
from jax.experimental import pallas as pl
from jax.experimental.pallas import tpu as pltpu
from jax.sharding import PartitionSpec as P

D = 2560
HALF = D // 2
HEADS = 20
HD = 128
CIN = 64
TOK = 256
PLANE = 32
CLIPS_HERE = 16
UNITS = 30
OWN = 5
BLOCK = 80
EPSILON = 1e-06
F32 = jnp.float32
BF16 = jnp.bfloat16
MESH = pl.DeviceIdType.MESH
HIGHEST = lax.Precision.HIGHEST


def unit_target(unit):
    is_query = unit < HEADS // 2
    pair = unit - HEADS // 2
    head = jnp.where(is_query, unit, pair // 2)
    core = head // OWN
    slot = head % OWN + jnp.where(is_query, 0, OWN + OWN * (pair % 2))
    return core, slot


def kernel(
    shape_ref,
    counts_ref,
    patches_ref,
    weight_ref,
    bias_ref,
    block_ref,
    time_ref,
    query_weight_ref,
    pair_weight_ref,
    query_bias_hbm,
    pair_bias_hbm,
    gain_hbm,
    out_ref,
    query_weight,
    pair_weight,
    query_bias_ref,
    pair_bias_ref,
    gain_ref,
    query_ref,
    pair_ref,
    tokens,
    weight_all,
    bias_all,
    block_all,
    time_all,
    centred,
    modulated,
    landed,
    columns,
    sending,
    units,
    rows_aug,
    scale_rows,
    cosines,
    sines,
    query_rows,
    key_rows,
    value_rows,
    valid_rows,
    query_acc,
    key_acc,
    sums_out,
    sums_in,
    result,
    send_a,
    recv_a,
    send_b,
    recv_b,
    send_c,
    recv_c,
    send_p,
    recv_p,
    send_s,
    recv_s,
    send_o,
    recv_o,
    local,
    local_o,
):
    s = lax.axis_index("seq")
    m = lax.axis_index("mp")
    x_lo = s // (2 * PLANE)
    chip = (s // 2) % PLANE
    core = s % 2
    other = 1 - core
    owner = chip < UNITS
    unit_core, unit_slot = unit_target(chip)
    crossing = jnp.logical_and(owner, unit_core != core)

    def plane_device(index, side):
        return (x_lo * 2 * PLANE + index * 2 + side, m)

    sibling = plane_device(chip, other)
    partner = (s, 1 - m)
    diagonal = (sibling[0], 1 - m)
    neighbour = (s + 2 * PLANE * (1 - 2 * x_lo), m)

    def remote(src, dst, send, recv, device):
        return pltpu.make_async_remote_copy(
            src_ref=src, dst_ref=dst, send_sem=send, recv_sem=recv, device_id=device, device_id_type=MESH
        )

    barrier = pltpu.get_barrier_semaphore()

    def greet(step, carry):
        pl.semaphore_signal(
            barrier, inc=1, device_id=plane_device((chip + step) % PLANE, core), device_id_type=MESH
        )
        return carry

    lax.fori_loop(1, PLANE, greet, 0)
    for device in (sibling, partner, diagonal, neighbour):
        pl.semaphore_signal(barrier, inc=1, device_id=device, device_id_type=MESH)

    @pl.when(chip // CLIPS_HERE != core)
    def _():
        def greet_owner(step, carry):
            unit = jnp.where(
                step < OWN, core * OWN + step, HEADS // 2 + core * 2 * OWN + step - OWN
            )
            pl.semaphore_signal(
                barrier, inc=1, device_id=plane_device(unit, other), device_id_type=MESH
            )
            return carry

        lax.fori_loop(0, 3 * OWN, greet_owner, 0)

    half_rows = pl.ds(pl.multiple_of(core * (CIN // 2), CIN // 2), CIN // 2)
    own_clips = pl.ds(x_lo * PLANE + core * CLIPS_HERE, CLIPS_HERE)

    weight_copies = [
        pltpu.make_async_copy(query_weight_ref, query_weight, local.at[0]),
        pltpu.make_async_copy(pair_weight_ref, pair_weight, local.at[1]),
    ]
    own_copies = [
        pltpu.make_async_copy(patches_ref, tokens.at[core], local.at[2]),
        pltpu.make_async_copy(weight_ref.at[pl.ds(0, CIN // 2)], weight_all.at[m, 0], local.at[3]),
        pltpu.make_async_copy(
            weight_ref.at[pl.ds(CIN // 2, CIN // 2)], weight_all.at[m, 1], local.at[4]
        ),
        pltpu.make_async_copy(bias_ref, bias_all.at[m, 0], local.at[5]),
        pltpu.make_async_copy(block_ref, block_all.at[m], local.at[6]),
        pltpu.make_async_copy(time_ref.at[own_clips], time_all.at[m], local.at[7]),
        pltpu.make_async_copy(query_bias_hbm, query_bias_ref.at[0], local.at[8]),
        pltpu.make_async_copy(pair_bias_hbm, pair_bias_ref.at[0], local.at[9]),
        pltpu.make_async_copy(gain_hbm, gain_ref, local.at[10]),
    ]
    for copy in weight_copies + own_copies:
        copy.start()

    units[:, BLOCK:, :] = jnp.zeros((3 * OWN, HD - BLOCK, HD), BF16)
    rows_aug[:, CIN:] = jnp.where(
        lax.broadcasted_iota(jnp.int32, (2 * TOK, HD - CIN), 1) < 2, 1.0, 0.0
    ).astype(BF16)
    for copy in weight_copies:
        copy.wait()
    query_ref[...] = query_weight[...].reshape(5, 4, HALF)
    pair_ref[...] = pair_weight[...].reshape(5, 4, D)

    clip = s // 2
    height = shape_ref[1, clip].astype(F32)
    width = shape_ref[2, clip].astype(F32)
    lane = lax.broadcasted_iota(jnp.int32, (1, HD), 1)
    other_pairs = HD // 6
    frame_pairs = HD // 2 - 2 * other_pairs
    pair_id = lane // 2
    in_frame = pair_id < frame_pairs
    in_row = jnp.logical_and(pair_id >= frame_pairs, pair_id < frame_pairs + other_pairs)
    within = jnp.where(
        in_frame,
        pair_id,
        jnp.where(in_row, pair_id - frame_pairs, pair_id - frame_pairs - other_pairs),
    ).astype(F32)
    axis_span = jnp.where(in_frame, 2.0 * frame_pairs, 2.0 * other_pairs).astype(F32)
    inverse = jnp.exp(-(2.0 * within / axis_span) * math.log(10000.0))
    even = lane % 2 == 0
    for part in range(2):
        slot = lax.broadcasted_iota(jnp.int32, (TOK, HD), 0)
        offset = counts_ref[2 * clip] if part else 0
        position = (slot + offset).astype(F32)
        line = jnp.floor((position + 0.5) / width)
        column_pos = position - line * width
        frame_pos = jnp.floor((line + 0.5) / height)
        row_pos = line - frame_pos * height
        angles = jnp.where(in_frame, frame_pos, jnp.where(in_row, row_pos, column_pos)) * inverse
        sine = jnp.sin(angles)
        cosines[part * TOK : (part + 1) * TOK, :] = jnp.cos(angles)
        sines[part * TOK : (part + 1) * TOK, :] = jnp.where(even, -sine, sine)
        valid = slot < counts_ref[2 * clip + part]
        kept = jnp.where(valid, 1.0, 0.0).astype(BF16)
        valid_rows[part * TOK : (part + 1) * TOK, :] = jnp.where(valid, 1.0, 0.0)
        for head in range(OWN):
            value_rows[head, part * TOK : (part + 1) * TOK, HD:] = kept

    pl.semaphore_wait(barrier, PLANE - 1 + 4 + jnp.where(crossing, CLIPS_HERE, 0))

    param_copies = [
        remote(patches_ref, tokens.at[core], send_p.at[0], recv_p.at[0], sibling),
        remote(weight_ref.at[half_rows], weight_all.at[m, core], send_p.at[1], recv_p.at[1], partner),
        remote(bias_ref, bias_all.at[m, 0], send_p.at[2], recv_p.at[2], partner),
        remote(block_ref, block_all.at[m], send_p.at[3], recv_p.at[3], partner),
        remote(time_ref.at[own_clips], time_all.at[m], send_p.at[4], recv_p.at[4], partner),
    ]
    for copy in param_copies:
        copy.start()

    def query_source(unit):
        return query_ref.at[:, :, pl.ds(pl.multiple_of(unit * HD, HD), HD)]

    def pair_source(unit):
        return pair_ref.at[:, :, pl.ds(pl.multiple_of((unit - HEADS // 2) * HD, HD), HD)]

    landing = landed.at[x_lo, chip, core]

    def scatter(step, carry):
        unit = (chip + step) % PLANE

        @pl.when(unit < HEADS // 2)
        def _():
            remote(
                query_source(unit), landing, send_a.at[step], recv_a.at[chip], plane_device(unit, core)
            ).start()

        @pl.when(jnp.logical_and(unit >= HEADS // 2, unit < UNITS))
        def _():
            remote(
                pair_source(unit), landing, send_a.at[step], recv_a.at[chip], plane_device(unit, core)
            ).start()

        return carry

    lax.fori_loop(1, PLANE, scatter, 0)

    @pl.when(chip < HEADS // 2)
    def _():
        pltpu.make_async_copy(query_source(chip), landing, recv_a.at[chip]).start()

    @pl.when(jnp.logical_and(chip >= HEADS // 2, owner))
    def _():
        pltpu.make_async_copy(pair_source(chip), landing, recv_a.at[chip]).start()

    here = landed.at[x_lo, :, core]
    there = landed.at[1 - x_lo, :, core]
    to_sibling = remote(here, here, send_b.at[0], recv_b.at[0], sibling)
    to_neighbour = remote(here, here, send_b.at[1], recv_b.at[1], neighbour)
    passed_on = remote(there, there, send_b.at[2], recv_b.at[2], sibling)

    @pl.when(owner)
    def _():
        pltpu.make_async_copy(landing, landing, recv_a.at[chip]).wait()

        def arrive(step, carry):
            source = (chip + step) % PLANE
            block = landed.at[x_lo, source, core]
            remote(
                block, block, send_a.at[0], recv_a.at[source], plane_device(source, core)
            ).wait_recv()
            return carry

        lax.fori_loop(1, PLANE, arrive, 0)
        to_neighbour.start()
        to_sibling.start()

    param_copies[1].wait_recv()
    weight_block = weight_all.at[1 - m, core]
    shared = remote(weight_block, weight_block, send_p.at[5], recv_p.at[5], sibling)
    shared.start()
    for copy in own_copies:
        copy.wait()
    for copy in param_copies[:1] + param_copies[2:] + [shared]:
        copy.wait_recv()
    for part in range(2):
        rows_aug[part * TOK : (part + 1) * TOK, 0:CIN] = tokens[part].T

    def statistics(step, carry):
        rows = pl.ds(pl.multiple_of(step * 128, 128), 128)
        patch = rows_aug[rows, 0:CIN]
        total = jnp.zeros((128, 1), F32)
        square = jnp.zeros((128, 1), F32)
        for half in range(2):
            embedded = jnp.dot(patch, weight_all[half].reshape(CIN, HALF), preferred_element_type=F32) + bias_all[half]
            total += jnp.sum(embedded, axis=1, keepdims=True)
            square += jnp.sum(embedded * embedded, axis=1, keepdims=True)
        average = total / D
        variance = square / D - average * average
        scale_rows[rows, :] = jnp.broadcast_to(lax.rsqrt(variance + EPSILON), (128, HD))
        return carry

    lax.fori_loop(0, 4, statistics, 0)

    row_mean = (
        jnp.sum(weight_all[0].reshape(CIN, HALF).astype(F32), axis=1, keepdims=True)
        + jnp.sum(weight_all[1].reshape(CIN, HALF).astype(F32), axis=1, keepdims=True)
    ) / D
    bias_mean = (
        jnp.sum(bias_all[0], axis=1, keepdims=True) + jnp.sum(bias_all[1], axis=1, keepdims=True)
    ) / D
    for half in range(2):
        centred[half] = weight_all[half].reshape(CIN, HALF).astype(F32) - row_mean

    def modulate(step, carry):
        rows = pl.multiple_of(step * BLOCK, 16)
        index = lax.broadcasted_iota(jnp.int32, (BLOCK - CIN, HALF), 0)
        for half in range(2):
            scale = 1.0 + time_all[half, step, 1:2, :] + block_all[half, 1:2, :]
            shift = time_all[half, step, 0:1, :] + block_all[half, 0:1, :]
            span = slice(half * HALF, (half + 1) * HALF)
            modulated[pl.ds(rows, CIN), span] = (centred[half] * scale).astype(BF16)
            bias_row = (bias_all[half] - bias_mean) * scale
            bias_low = bias_row - bias_row.astype(BF16).astype(F32)
            shift_low = shift - shift.astype(BF16).astype(F32)
            extra = jnp.where(
                index == 0,
                bias_row,
                jnp.where(
                    index == 1,
                    bias_low,
                    jnp.where(index == 2, shift, jnp.where(index == 3, shift_low, 0.0)),
                ),
            )
            modulated[pl.ds(pl.multiple_of(rows + CIN, 16), BLOCK - CIN), span] = extra.astype(BF16)
        return carry

    lax.fori_loop(0, CLIPS_HERE, modulate, 0)

    @pl.when(owner)
    def _():
        to_neighbour.wait_recv()
        passed_on.start()
        to_sibling.wait_recv()
        passed_on.wait_recv()
        columns[...] = landed[...].reshape(D, HD)

        for turn in range(4):
            chunk = (turn + chip) % 4
            folded = jnp.dot(
                modulated[pl.ds(pl.multiple_of(chunk * 4 * BLOCK, 4 * BLOCK), 4 * BLOCK), :],
                columns[...],
                preferred_element_type=F32,
            )
            for piece in range(4):
                target = chunk * 4 + piece
                block = folded[piece * BLOCK : (piece + 1) * BLOCK]
                extra = block[CIN:]
                bias_row = extra[0:1] + extra[1:2]
                shift_row = extra[2:3] + extra[3:4]
                index = lax.broadcasted_iota(jnp.int32, (BLOCK - CIN, HD), 0)
                tail = jnp.where(
                    index == 0,
                    bias_row,
                    jnp.where(
                        index == 1,
                        bias_row - bias_row.astype(BF16).astype(F32),
                        jnp.where(
                            index == 2,
                            shift_row,
                            jnp.where(
                                index == 3, shift_row - shift_row.astype(BF16).astype(F32), 0.0
                            ),
                        ),
                    ),
                )
                sending[target, 0:CIN, :] = block[:CIN].astype(BF16)
                sending[target, CIN:, :] = tail.astype(BF16)

            for piece in range(4):
                target = chunk * 4 + (piece + chip // 4) % 4
                device = plane_device(core * CLIPS_HERE + target, unit_core)

                @pl.when(device[0] != s)
                def _():
                    remote(
                        sending.at[target],
                        units.at[unit_slot, pl.ds(0, BLOCK)],
                        send_c.at[target],
                        recv_c.at[unit_slot],
                        device,
                    ).start()

                @pl.when(device[0] == s)
                def _():
                    pltpu.make_async_copy(
                        sending.at[target], units.at[unit_slot, pl.ds(0, BLOCK)], recv_c.at[unit_slot]
                    ).start()

    def collect(slot, carry):
        block = units.at[slot, pl.ds(0, BLOCK)]
        pltpu.make_async_copy(block, block, recv_c.at[slot]).wait()
        return carry

    query_acc[...] = jnp.zeros_like(query_acc)
    key_acc[...] = jnp.zeros_like(key_acc)

    def unit_rows(slot):
        unit = units[slot]
        shift_row = unit[CIN + 2 : CIN + 3].astype(F32) + unit[CIN + 3 : CIN + 4].astype(F32)
        return unit, shift_row

    def rotated(values, rows):
        partner_rows = jnp.where(even, pltpu.roll(values, HD - 1, 1), pltpu.roll(values, 1, 1))
        return values * cosines[rows, :] + partner_rows * sines[rows, :]

    lax.fori_loop(0, 2 * OWN, collect, 0)

    def project(head, carry):
        column = pl.multiple_of((core * OWN + head) * HD, HD)
        query_unit, query_shift = unit_rows(head)
        key_unit, key_shift = unit_rows(OWN + head)
        both = jnp.concatenate([query_unit, key_unit], axis=1)
        query_shift += query_bias_ref[0:1, pl.ds(column, HD)]
        key_shift += pair_bias_ref[0:1, pl.ds(pl.multiple_of(column * 2, HD), HD)]
        for part in range(2):
            rows = slice(part * TOK, (part + 1) * TOK)
            product = jnp.dot(rows_aug[rows, :], both, preferred_element_type=F32)
            scale = scale_rows[rows, :]
            raw = product[:, :HD] * scale + query_shift
            query_acc[rows, :] += raw * raw
            query_rows[head, rows, :] = raw
            raw = product[:, HD:] * scale + key_shift
            key_acc[rows, :] += raw * raw
            key_rows[head, rows, :] = raw
        return carry

    lax.fori_loop(0, OWN, project, 0)

    ones = jnp.ones((8, HD), F32)
    contract_lanes = (((1,), (1,)), ((), ()))
    contract_rows = (((0,), (0,)), ((), ()))
    query_sums = lax.dot_general(
        ones, query_acc[...], contract_lanes, precision=HIGHEST, preferred_element_type=F32
    )
    key_sums = lax.dot_general(
        ones, key_acc[...], contract_lanes, precision=HIGHEST, preferred_element_type=F32
    )
    sum_index = lax.broadcasted_iota(jnp.int32, (8, 2 * TOK), 0)
    sums_out[...] = jnp.where(sum_index == 0, query_sums, key_sums)
    sum_copies = [
        remote(sums_out, sums_in.at[0], send_s.at[0], recv_s.at[0], sibling),
        remote(sums_out, sums_in.at[1], send_s.at[1], recv_s.at[1], partner),
        remote(
            sums_out,
            sums_in.at[2],
            send_s.at[2],
            recv_s.at[2],
            diagonal,
        ),
    ]
    for copy in sum_copies:
        copy.start()

    def rotate(head, carry):
        column = pl.multiple_of((core * OWN + head) * HD, HD)
        query_gain = gain_ref[0:1, pl.ds(column, HD)]
        key_gain = gain_ref[1:2, pl.ds(column, HD)]
        for part in range(2):
            rows = slice(part * TOK, (part + 1) * TOK)
            query_rows[head, rows, :] = rotated(query_rows[head, rows, :] * query_gain, rows)
            key_rows[head, rows, :] = rotated(key_rows[head, rows, :] * key_gain, rows)
        return carry

    lax.fori_loop(0, OWN, rotate, 0)

    def collect_value(head, carry):
        return collect(2 * OWN + head, carry)

    lax.fori_loop(0, OWN, collect_value, 0)

    def values(head, carry):
        column = pl.multiple_of(((core * OWN + head) * 2 + 1) * HD, HD)
        unit, shift = unit_rows(2 * OWN + head)
        shift += pair_bias_ref[0:1, pl.ds(column, HD)]
        for part in range(2):
            rows = slice(part * TOK, (part + 1) * TOK)
            product = jnp.dot(rows_aug[rows, :], unit, preferred_element_type=F32)
            raw = product * scale_rows[rows, :] + shift
            value_rows[head, rows, :HD] = jnp.where(valid_rows[rows, :] > 0.0, raw, 0.0).astype(BF16)
        return carry

    lax.fori_loop(0, OWN, values, 0)

    for copy in sum_copies:
        copy.wait_recv()
    square_sums = sums_out[...] + sums_in[0] + sums_in[1] + sums_in[2]
    factors = lax.rsqrt(square_sums / (HEADS * HD) + EPSILON)
    query_factor = lax.dot_general(
        jnp.where(sum_index == 0, factors * (HD**-0.5 * math.log2(math.e)), 0.0),
        ones,
        contract_rows,
        precision=HIGHEST,
        preferred_element_type=F32,
    )
    key_factor = lax.dot_general(
        jnp.where(sum_index == 1, factors, 0.0),
        ones,
        contract_rows,
        precision=HIGHEST,
        preferred_element_type=F32,
    )
    query_acc[...] = query_factor
    key_acc[...] = jnp.where(valid_rows[...] > 0.0, key_factor, 0.0)

    def own_result(head):
        span = pl.ds(pl.multiple_of((core * OWN + head) * HD, HD), HD)
        return pltpu.make_async_copy(result.at[core, head], out_ref.at[:, span], local_o.at[head])

    def other_result(head):
        span = pl.ds(pl.multiple_of((core * OWN + head) * HD, HD), HD)
        return remote(
            result.at[other, head], out_ref.at[:, span], send_o.at[head], recv_o.at[head], sibling
        )

    def attend(head, carry):
        keys = (key_rows[head] * key_acc[...]).astype(BF16)
        for part in range(2):
            rows = slice(part * TOK, (part + 1) * TOK)
            queries = (query_rows[head, rows, :] * query_acc[rows, :]).astype(BF16)
            scores = lax.dot_general(queries, keys, contract_lanes, preferred_element_type=F32)
            weights = jnp.exp2(scores).astype(BF16)
            summed = jnp.dot(weights, value_rows[head], preferred_element_type=F32)
            kept = jnp.where(valid_rows[rows, :] > 0.0, summed[:, :HD] / summed[:, HD:], 0.0)
            result[part, head] = kept.astype(BF16)
        other_result(head).start()
        own_result(head).start()
        return carry

    lax.fori_loop(0, OWN, attend, 0)

    for head in range(OWN):
        span = pl.ds(pl.multiple_of((other * OWN + head) * HD, HD), HD)
        arrived = out_ref.at[:, span]
        remote(arrived, arrived, send_o.at[head], recv_o.at[head], sibling).wait_recv()
        other_result(head).wait_send()
        own_result(head).wait()

    for copy in param_copies + [shared] + sum_copies:
        copy.wait_send()

    def sent(step, carry):
        @pl.when((chip + step) % PLANE < UNITS)
        def _():
            remote(query_source(0), landing, send_a.at[step], recv_a.at[chip], partner).wait_send()

        return carry

    lax.fori_loop(1, PLANE, sent, 0)

    @pl.when(owner)
    def _():
        for copy in (to_sibling, to_neighbour, passed_on):
            copy.wait_send()

        def sent_block(target, carry):
            @pl.when(plane_device(core * CLIPS_HERE + target, unit_core)[0] != s)
            def _():
                remote(
                    sending.at[target],
                    units.at[unit_slot, pl.ds(0, BLOCK)],
                    send_c.at[target],
                    recv_c.at[unit_slot],
                    partner,
                ).wait_send()

            return carry

        lax.fori_loop(0, CLIPS_HERE, sent_block, 0)


def shards(
    patches,
    clip_shape,
    shard_counts,
    patch_weight,
    patch_bias,
    time_mod,
    block_mod,
    w_query,
    query_bias,
    w_keyvalue,
    keyvalue_bias,
    norm_gain,
):
    smem = pl.BlockSpec(memory_space=pltpu.SMEM)
    anywhere = pl.BlockSpec(memory_space=pl.ANY)
    dma = pltpu.SemaphoreType.DMA
    return pl.pallas_call(
        kernel,
        out_shape=jax.ShapeDtypeStruct((TOK, HALF), BF16),
        in_specs=[smem, smem] + [anywhere] * 10,
        out_specs=anywhere,
        scratch_shapes=[
            pltpu.VMEM((20, HALF), BF16),
            pltpu.VMEM((20, D), BF16),
            pltpu.VMEM((1, HALF), F32),
            pltpu.VMEM((1, D), F32),
            pltpu.VMEM((2, HALF), F32),
            pltpu.VMEM((5, 4, HALF), BF16),
            pltpu.VMEM((5, 4, D), BF16),
            pltpu.VMEM((2, CIN, TOK), BF16),
            pltpu.VMEM((2, 2, CIN // 2, HALF), BF16),
            pltpu.VMEM((2, 1, HALF), F32),
            pltpu.VMEM((2, 2, HALF), F32),
            pltpu.VMEM((2, CLIPS_HERE, 2, HALF), F32),
            pltpu.VMEM((2, CIN, HALF), F32),
            pltpu.VMEM((CLIPS_HERE * BLOCK, D), BF16),
            pltpu.VMEM((2, PLANE, 2, 5, 4, HD), BF16),
            pltpu.VMEM((D, HD), BF16),
            pltpu.VMEM((CLIPS_HERE, BLOCK, HD), BF16),
            pltpu.VMEM((3 * OWN, HD, HD), BF16),
            pltpu.VMEM((2 * TOK, HD), BF16),
            pltpu.VMEM((2 * TOK, HD), F32),
            pltpu.VMEM((2 * TOK, HD), F32),
            pltpu.VMEM((2 * TOK, HD), F32),
            pltpu.VMEM((OWN, 2 * TOK, HD), F32),
            pltpu.VMEM((OWN, 2 * TOK, HD), F32),
            pltpu.VMEM((OWN, 2 * TOK, 2 * HD), BF16),
            pltpu.VMEM((2 * TOK, HD), F32),
            pltpu.VMEM((2 * TOK, HD), F32),
            pltpu.VMEM((2 * TOK, HD), F32),
            pltpu.VMEM((8, 2 * TOK), F32),
            pltpu.VMEM((3, 8, 2 * TOK), F32),
            pltpu.VMEM((2, OWN, TOK, HD), BF16),
            dma((PLANE,)),
            dma((PLANE,)),
            dma((3,)),
            dma((3,)),
            dma((CLIPS_HERE,)),
            dma((3 * OWN,)),
            dma((6,)),
            dma((6,)),
            dma((3,)),
            dma((3,)),
            dma((OWN,)),
            dma((OWN,)),
            dma((11,)),
            dma((OWN,)),
        ],
        compiler_params=pltpu.CompilerParams(
            collective_id=0, has_side_effects=True, vmem_limit_bytes=60 << 20
        ),
    )(
        clip_shape.T,
        shard_counts,
        patches.T,
        patch_weight,
        patch_bias,
        block_mod,
        time_mod,
        w_query,
        w_keyvalue,
        query_bias,
        keyvalue_bias,
        norm_gain,
    )


def solution(mesh):
    return jax.shard_map(
        shards,
        mesh=mesh,
        in_specs=(
            P("seq", None),
            P(),
            P(),
            P(None, "mp"),
            P("mp"),
            P(None, None, "mp"),
            P(None, "mp"),
            P("seq", "mp"),
            P("mp"),
            P("seq", "mp"),
            P("mp"),
            P(None, "mp"),
        ),
        out_specs=P("seq", "mp"),
        check_vma=False,
    )
```

```python
import functools
import math

import jax
import jax.numpy as jnp
from jax import lax
from jax.experimental import pallas as pl
from jax.experimental.pallas import tpu as pltpu
from jax.sharding import PartitionSpec as P

D = 2560
HALF = D // 2
HEADS = 20
HD = 128
CIN = 64
TOK = 256
PLANE = 32
CLIPS_HERE = 16
UNITS = 30
OWN = 5
GROUPS = 8
BLOCK = 80
WIRE = 72
EPSILON = 1e-06
F32 = jnp.float32
BF16 = jnp.bfloat16
MESH = pl.DeviceIdType.MESH


def unit_target(unit):
    is_query = unit < HEADS // 2
    pair = unit - HEADS // 2
    head = jnp.where(is_query, unit, pair // 2)
    core = head // OWN
    slot = head % OWN + jnp.where(is_query, 0, OWN + OWN * (pair % 2))
    return core, slot


def kernel(
    shape_ref,
    counts_ref,
    patches_ref,
    weight_ref,
    bias_ref,
    block_ref,
    time_ref,
    query_weight_ref,
    pair_weight_ref,
    query_bias_hbm,
    pair_bias_hbm,
    gain_hbm,
    out_ref,
    query_weight,
    pair_weight,
    query_bias_ref,
    pair_bias_ref,
    gain_ref,
    rows_ref,
    tokens,
    weight_all,
    bias_all,
    block_all,
    time_all,
    row_sums,
    row_sums_in,
    centred,
    modulated,
    landed,
    columns,
    sending,
    units,
    rows_aug,
    scale_rows,
    cosines,
    sines,
    query_rows,
    key_rows,
    value_rows,
    valid_rows,
    query_acc,
    key_acc,
    sums_out,
    sums_in,
    result,
    send_a,
    recv_a,
    send_b,
    recv_b,
    send_c,
    recv_c,
    send_p,
    recv_p,
    send_s,
    recv_s,
    send_o,
    recv_o,
    local,
    local_o,
):
    s = lax.axis_index("seq")
    m = lax.axis_index("mp")
    x_lo = s // (2 * PLANE)
    chip = (s // 2) % PLANE
    core = s % 2
    other = 1 - core
    owner = chip < UNITS
    unit_core, unit_slot = unit_target(chip)
    crossing = jnp.logical_and(owner, unit_core != core)

    def plane_device(index, side):
        return (x_lo * 2 * PLANE + index * 2 + side, m)

    sibling = plane_device(chip, other)
    partner = (s, 1 - m)
    diagonal = (sibling[0], 1 - m)
    neighbour = (s + 2 * PLANE * (1 - 2 * x_lo), m)
    adjacent = (neighbour[0], 1 - m)

    def remote(src, dst, send, recv, device):
        return pltpu.make_async_remote_copy(
            src_ref=src, dst_ref=dst, send_sem=send, recv_sem=recv, device_id=device, device_id_type=MESH
        )

    barrier = pltpu.get_barrier_semaphore()

    def far_first(index):
        return PLANE // 2 + (1 - 2 * (index % 2)) * ((index + 1) // 2)

    def greet(index, carry):
        step = far_first(index)
        pl.semaphore_signal(
            barrier, inc=1, device_id=plane_device((chip + step) % PLANE, core), device_id_type=MESH
        )
        return carry

    lax.fori_loop(0, PLANE - 1, greet, 0)
    for device in (neighbour, adjacent, partner, diagonal, sibling):
        pl.semaphore_signal(barrier, inc=1, device_id=device, device_id_type=MESH)

    @pl.when(chip // CLIPS_HERE != core)
    def _():
        def greet_owner(step, carry):
            unit = jnp.where(
                step < OWN, core * OWN + step, HEADS // 2 + core * 2 * OWN + step - OWN
            )
            pl.semaphore_signal(
                barrier, inc=1, device_id=plane_device(unit, other), device_id_type=MESH
            )
            return carry

        lax.fori_loop(0, 3 * OWN, greet_owner, 0)

    half_rows = pl.ds(pl.multiple_of(core * (CIN // 2), CIN // 2), CIN // 2)
    own_clips = pl.ds(x_lo * PLANE + core * CLIPS_HERE, CLIPS_HERE)
    adjacent_clips = pl.ds((1 - x_lo) * PLANE + core * CLIPS_HERE, CLIPS_HERE)

    weight_copies = [
        pltpu.make_async_copy(query_weight_ref, query_weight, local.at[0]),
        pltpu.make_async_copy(pair_weight_ref, pair_weight, local.at[1]),
    ]
    own_copies = [
        pltpu.make_async_copy(patches_ref, tokens.at[core], local.at[2]),
        pltpu.make_async_copy(weight_ref.at[pl.ds(0, CIN // 2)], weight_all.at[m, 0], local.at[3]),
        pltpu.make_async_copy(
            weight_ref.at[pl.ds(CIN // 2, CIN // 2)], weight_all.at[m, 1], local.at[4]
        ),
        pltpu.make_async_copy(bias_ref, bias_all.at[m, 0], local.at[5]),
        pltpu.make_async_copy(block_ref, block_all.at[m], local.at[6]),
        pltpu.make_async_copy(time_ref.at[own_clips], time_all.at[m], local.at[7]),
        pltpu.make_async_copy(query_bias_hbm, query_bias_ref.at[0], local.at[8]),
        pltpu.make_async_copy(pair_bias_hbm, pair_bias_ref.at[0], local.at[9]),
        pltpu.make_async_copy(gain_hbm, gain_ref, local.at[10]),
    ]
    for copy in weight_copies + own_copies:
        copy.start()

    units[:, WIRE:, :] = jnp.zeros((3 * OWN, HD - WIRE, HD), BF16)
    rows_aug[:, CIN:] = jnp.where(
        lax.broadcasted_iota(jnp.int32, (2 * TOK, HD - CIN), 1) < 2, 1.0, 0.0
    ).astype(BF16)
    for copy in weight_copies:
        copy.wait()
    rows_ref[:, :, :HALF] = query_weight[...].reshape(5, 4, HALF)
    rows_ref[:, :, HALF:] = pair_weight[...].reshape(5, 4, D)

    clip = s // 2
    height = shape_ref[1, clip].astype(F32)
    width = shape_ref[2, clip].astype(F32)
    lane = lax.broadcasted_iota(jnp.int32, (1, HD), 1)
    other_pairs = HD // 6
    frame_pairs = HD // 2 - 2 * other_pairs
    pair_id = lane // 2
    in_frame = pair_id < frame_pairs
    in_row = jnp.logical_and(pair_id >= frame_pairs, pair_id < frame_pairs + other_pairs)
    within = jnp.where(
        in_frame,
        pair_id,
        jnp.where(in_row, pair_id - frame_pairs, pair_id - frame_pairs - other_pairs),
    ).astype(F32)
    axis_span = jnp.where(in_frame, 2.0 * frame_pairs, 2.0 * other_pairs).astype(F32)
    inverse = jnp.exp(-(2.0 * within / axis_span) * math.log(10000.0))
    even = lane % 2 == 0
    for part in range(2):
        slot = lax.broadcasted_iota(jnp.int32, (TOK, HD), 0)
        offset = counts_ref[2 * clip] if part else 0
        position = (slot + offset).astype(F32)
        line = jnp.floor((position + 0.5) / width)
        column_pos = position - line * width
        frame_pos = jnp.floor((line + 0.5) / height)
        row_pos = line - frame_pos * height
        angles = jnp.where(in_frame, frame_pos, jnp.where(in_row, row_pos, column_pos)) * inverse
        sine = jnp.sin(angles)
        cosines[part * TOK : (part + 1) * TOK, :] = jnp.cos(angles)
        sines[part * TOK : (part + 1) * TOK, :] = jnp.where(even, -sine, sine)
        valid = slot < counts_ref[2 * clip + part]
        kept = jnp.where(valid, 1.0, 0.0).astype(BF16)
        valid_rows[part * TOK : (part + 1) * TOK, :] = jnp.where(valid, 1.0, 0.0)
        for head in range(OWN):
            value_rows[head, part * TOK : (part + 1) * TOK, HD:] = kept

    for copy in own_copies:
        copy.wait()
    for part in range(2):
        block_rows = slice(part * CIN // 2, (part + 1) * CIN // 2)
        row_sums[block_rows, :] = jnp.broadcast_to(
            jnp.sum(weight_all[m, part].astype(F32), axis=1, keepdims=True), (CIN // 2, HD)
        )
    row_sums[CIN:, :] = jnp.broadcast_to(jnp.sum(bias_all[m], axis=1, keepdims=True), (8, HD))

    pl.semaphore_wait(barrier, PLANE - 1 + 5 + jnp.where(crossing, CLIPS_HERE, 0))

    param_copies = [
        remote(patches_ref, tokens.at[core], send_p.at[0], recv_p.at[0], sibling),
        remote(weight_ref.at[half_rows], weight_all.at[m, core], send_p.at[1], recv_p.at[1], adjacent),
        remote(bias_ref, bias_all.at[m, 0], send_p.at[2], recv_p.at[2], adjacent),
        remote(block_ref, block_all.at[m], send_p.at[3], recv_p.at[3], adjacent),
        remote(time_ref.at[adjacent_clips], time_all.at[m], send_p.at[4], recv_p.at[4], adjacent),
    ]
    def source_of(unit):
        return rows_ref.at[:, :, pl.ds(pl.multiple_of(unit * HD, HD), HD)]

    landing = landed.at[x_lo, chip, core]

    def scatter(index, carry):
        step = far_first(index)
        unit = (chip + step) % PLANE

        @pl.when(unit < UNITS)
        def _():
            remote(
                source_of(unit), landing, send_a.at[step], recv_a.at[chip], plane_device(unit, core)
            ).start()

        return carry

    lax.fori_loop(0, PLANE - 1, scatter, 0)

    @pl.when(owner)
    def _():
        pltpu.make_async_copy(source_of(chip), landing, recv_a.at[chip]).start()

    sums_copy = remote(row_sums, row_sums_in, send_p.at[6], recv_p.at[6], adjacent)
    sums_copy.start()
    for copy in param_copies:
        copy.start()

    depth = chip // 4

    def group_of(index):
        return pl.ds((depth + (0, 1, 7, 2, 6, 3, 5, 4)[index]) % GROUPS * 4, 4)

    def to_sibling(index):
        block = landed.at[x_lo, group_of(index), core]
        return remote(block, block, send_b.at[index], recv_b.at[index], sibling)

    def to_neighbour(index):
        block = landed.at[x_lo, group_of(index), core]
        slot = GROUPS + index
        return remote(block, block, send_b.at[slot], recv_b.at[slot], neighbour)

    def passed_on(index):
        block = landed.at[1 - x_lo, group_of(index), core]
        slot = 2 * GROUPS + index
        return remote(block, block, send_b.at[slot], recv_b.at[slot], sibling)

    def hand_on(groups):
        @pl.when(owner)
        def _():
            for index in groups:
                first = (depth + (0, 1, 7, 2, 6, 3, 5, 4)[index]) % GROUPS * 4
                for step in range(4):
                    block = landed.at[x_lo, first + step, core]
                    pltpu.make_async_copy(block, block, recv_a.at[first + step]).wait()
                to_neighbour(index).start()
                to_sibling(index).start()

    def modulate_half(half):
        mean = (row_sums[:, 0:1] + row_sums_in[:, 0:1]) / D
        centred[...] = weight_all[half].reshape(CIN, HALF).astype(F32) - mean[:CIN]
        bias_row = bias_all[half] - mean[CIN : CIN + 1]
        span = pl.ds(pl.multiple_of(half * HALF, HALF), HALF)

        def modulate(step, carry):
            rows = pl.multiple_of(step * BLOCK, 16)
            index = lax.broadcasted_iota(jnp.int32, (BLOCK - CIN, HALF), 0)
            scale = 1.0 + time_all[half, step, 1:2, :] + block_all[half, 1:2, :]
            shift = time_all[half, step, 0:1, :] + block_all[half, 0:1, :]
            modulated[pl.ds(rows, CIN), span] = (centred[...] * scale).astype(BF16)
            bias_scaled = bias_row * scale
            bias_low = bias_scaled - bias_scaled.astype(BF16).astype(F32)
            shift_low = shift - shift.astype(BF16).astype(F32)
            extra = jnp.where(
                index == 0,
                bias_scaled,
                jnp.where(
                    index == 1,
                    bias_low,
                    jnp.where(index == 2, shift, jnp.where(index == 3, shift_low, 0.0)),
                ),
            )
            modulated[pl.ds(pl.multiple_of(rows + CIN, 16), BLOCK - CIN), span] = extra.astype(BF16)
            return carry

        lax.fori_loop(0, CLIPS_HERE, modulate, 0)

    hand_on(range(0, 3))
    sums_copy.wait_recv()
    modulate_half(m)
    hand_on(range(3, GROUPS))

    param_copies[1].wait_recv()
    weight_block = weight_all.at[1 - m, core]
    shared = remote(weight_block, weight_block, send_p.at[5], recv_p.at[5], sibling)
    shared.start()

    @pl.when(owner)
    def _():
        for index in range(GROUPS):
            to_neighbour(index).wait_recv()
            passed_on(index).start()

    for copy in param_copies[:1] + param_copies[2:] + [shared]:
        copy.wait_recv()
    modulate_half(1 - m)

    @pl.when(owner)
    def _():
        for index in range(GROUPS):
            to_sibling(index).wait_recv()
            passed_on(index).wait_recv()
        columns[...] = landed[...].reshape(D, HD)

        ahead = (core * 4 - depth) % GROUPS
        backward = jnp.logical_or(ahead <= 2, ahead == 7)
        for turn in range(4):
            chunk = jnp.where(backward, 3 - turn, turn)
            folded = jnp.dot(
                modulated[pl.ds(pl.multiple_of(chunk * 4 * BLOCK, 4 * BLOCK), 4 * BLOCK), :],
                columns[...],
                preferred_element_type=F32,
            )
            for piece in range(4):
                target = chunk * 4 + piece
                block = folded[piece * BLOCK : (piece + 1) * BLOCK]
                extra = block[CIN:]
                bias_row = extra[0:1] + extra[1:2]
                shift_row = extra[2:3] + extra[3:4]
                index = lax.broadcasted_iota(jnp.int32, (BLOCK - CIN, HD), 0)
                tail = jnp.where(
                    index == 0,
                    bias_row,
                    jnp.where(
                        index == 1,
                        bias_row - bias_row.astype(BF16).astype(F32),
                        jnp.where(
                            index == 2,
                            shift_row,
                            jnp.where(
                                index == 3, shift_row - shift_row.astype(BF16).astype(F32), 0.0
                            ),
                        ),
                    ),
                )
                sending[target, 0:CIN, :] = block[:CIN].astype(BF16)
                sending[target, CIN:, :] = tail.astype(BF16)

            for piece in range(4):
                target = chunk * 4 + (piece + chip // 4) % 4
                device = plane_device(core * CLIPS_HERE + target, unit_core)

                @pl.when(device[0] != s)
                def _():
                    remote(
                        sending.at[target, pl.ds(0, WIRE)],
                        units.at[unit_slot, pl.ds(0, WIRE)],
                        send_c.at[target],
                        recv_c.at[unit_slot],
                        device,
                    ).start()

                @pl.when(device[0] == s)
                def _():
                    pltpu.make_async_copy(
                        sending.at[target, pl.ds(0, WIRE)], units.at[unit_slot, pl.ds(0, WIRE)], recv_c.at[unit_slot]
                    ).start()


    for part in range(2):
        rows_aug[part * TOK : (part + 1) * TOK, 0:CIN] = tokens[part].T

    def statistics(step, carry):
        rows = pl.ds(pl.multiple_of(step * 128, 128), 128)
        patch = rows_aug[rows, 0:CIN]
        total = jnp.zeros((128, 1), F32)
        square = jnp.zeros((128, 1), F32)
        for half in range(2):
            embedded = (
                jnp.dot(patch, weight_all[half].reshape(CIN, HALF), preferred_element_type=F32)
                + bias_all[half]
            )
            total += jnp.sum(embedded, axis=1, keepdims=True)
            square += jnp.sum(embedded * embedded, axis=1, keepdims=True)
        average = total / D
        variance = square / D - average * average
        scale_rows[rows, :] = jnp.broadcast_to(lax.rsqrt(variance + EPSILON), (128, HD))
        return carry

    lax.fori_loop(0, 4, statistics, 0)

    def collect(slot, carry):
        block = units.at[slot, pl.ds(0, WIRE)]
        pltpu.make_async_copy(block, block, recv_c.at[slot]).wait()
        return carry

    query_acc[...] = jnp.zeros_like(query_acc)
    key_acc[...] = jnp.zeros_like(key_acc)

    def unit_rows(slot):
        unit = units[slot]
        shift_row = unit[CIN + 2 : CIN + 3].astype(F32) + unit[CIN + 3 : CIN + 4].astype(F32)
        return unit, shift_row

    def rotated(values, rows):
        partner_rows = jnp.where(even, pltpu.roll(values, HD - 1, 1), pltpu.roll(values, 1, 1))
        return values * cosines[rows, :] + partner_rows * sines[rows, :]

    lax.fori_loop(0, 2 * OWN, collect, 0)

    def project(head, carry):
        column = pl.multiple_of((core * OWN + head) * HD, HD)
        query_unit, query_shift = unit_rows(head)
        key_unit, key_shift = unit_rows(OWN + head)
        both = jnp.concatenate([query_unit, key_unit], axis=1)
        query_shift += query_bias_ref[0:1, pl.ds(column, HD)]
        key_shift += pair_bias_ref[0:1, pl.ds(pl.multiple_of(column * 2, HD), HD)]
        for part in range(2):
            rows = slice(part * TOK, (part + 1) * TOK)
            product = jnp.dot(rows_aug[rows, :], both, preferred_element_type=F32)
            scale = scale_rows[rows, :]
            raw = product[:, :HD] * scale + query_shift
            query_acc[rows, :] += raw * raw
            query_rows[head, rows, :] = raw
            raw = product[:, HD:] * scale + key_shift
            key_acc[rows, :] += raw * raw
            key_rows[head, rows, :] = raw
        return carry

    lax.fori_loop(0, OWN, project, 0)

    ones = jnp.ones((16, 2 * HD), BF16)
    contract_lanes = (((1,), (1,)), ((), ()))
    contract_rows = (((0,), (0,)), ((), ()))

    def split_sums(values):
        high = values.astype(BF16)
        low = (values - high.astype(F32)).astype(BF16)
        both = jnp.concatenate([high, low], axis=1)
        return lax.dot_general(ones, both, contract_lanes, preferred_element_type=F32)[:8]

    def split_columns(row):
        high = row.astype(BF16).astype(F32)
        middle = (row - high).astype(BF16).astype(F32)
        low = row - high - middle
        index = lax.broadcasted_iota(jnp.int32, (16, 2 * TOK), 0)
        parts = jnp.where(
            index == 0, high, jnp.where(index == 1, middle, jnp.where(index == 2, low, 0.0))
        ).astype(BF16)
        return lax.dot_general(parts, ones[:, :HD], contract_rows, preferred_element_type=F32)

    query_sums = split_sums(query_acc[...])
    key_sums = split_sums(key_acc[...])
    sum_index = lax.broadcasted_iota(jnp.int32, (8, 2 * TOK), 0)
    sums_out[...] = jnp.where(sum_index == 0, query_sums, key_sums)
    sum_copies = [
        remote(sums_out, sums_in.at[0], send_s.at[0], recv_s.at[0], sibling),
        remote(sums_out, sums_in.at[1], send_s.at[1], recv_s.at[1], partner),
        remote(
            sums_out,
            sums_in.at[2],
            send_s.at[2],
            recv_s.at[2],
            diagonal,
        ),
    ]
    for copy in sum_copies:
        copy.start()

    def rotate(head, carry):
        column = pl.multiple_of((core * OWN + head) * HD, HD)
        query_gain = gain_ref[0:1, pl.ds(column, HD)]
        key_gain = gain_ref[1:2, pl.ds(column, HD)]
        for part in range(2):
            rows = slice(part * TOK, (part + 1) * TOK)
            query_rows[head, rows, :] = rotated(query_rows[head, rows, :] * query_gain, rows)
            key_rows[head, rows, :] = rotated(key_rows[head, rows, :] * key_gain, rows)
        return carry

    lax.fori_loop(0, OWN, rotate, 0)

    def collect_value(head, carry):
        return collect(2 * OWN + head, carry)

    lax.fori_loop(0, OWN, collect_value, 0)

    def values(head, carry):
        column = pl.multiple_of(((core * OWN + head) * 2 + 1) * HD, HD)
        unit, shift = unit_rows(2 * OWN + head)
        shift += pair_bias_ref[0:1, pl.ds(column, HD)]
        for part in range(2):
            rows = slice(part * TOK, (part + 1) * TOK)
            product = jnp.dot(rows_aug[rows, :], unit, preferred_element_type=F32)
            raw = product * scale_rows[rows, :] + shift
            value_rows[head, rows, :HD] = jnp.where(valid_rows[rows, :] > 0.0, raw, 0.0).astype(BF16)
        return carry

    lax.fori_loop(0, OWN, values, 0)

    for copy in sum_copies:
        copy.wait_recv()
    square_sums = sums_out[...] + sums_in[0] + sums_in[1] + sums_in[2]
    factors = lax.rsqrt(square_sums / (HEADS * HD) + EPSILON)
    query_factor = split_columns(factors[0:1] * (HD**-0.5 * math.log2(math.e)))
    key_factor = split_columns(factors[1:2])
    query_acc[...] = query_factor
    key_acc[...] = jnp.where(valid_rows[...] > 0.0, key_factor, 0.0)

    def own_result(head):
        span = pl.ds(pl.multiple_of((core * OWN + head) * HD, HD), HD)
        return pltpu.make_async_copy(result.at[core, head], out_ref.at[:, span], local_o.at[head])

    def other_result(head):
        span = pl.ds(pl.multiple_of((core * OWN + head) * HD, HD), HD)
        return remote(
            result.at[other, head], out_ref.at[:, span], send_o.at[head], recv_o.at[head], sibling
        )

    def attend(head, carry):
        keys = (key_rows[head] * key_acc[...]).astype(BF16)
        for part in range(2):
            rows = slice(part * TOK, (part + 1) * TOK)
            queries = (query_rows[head, rows, :] * query_acc[rows, :]).astype(BF16)
            scores = lax.dot_general(queries, keys, contract_lanes, preferred_element_type=F32)
            weights = jnp.exp2(scores).astype(BF16)
            summed = jnp.dot(weights, value_rows[head], preferred_element_type=F32)
            kept = jnp.where(valid_rows[rows, :] > 0.0, summed[:, :HD] / summed[:, HD:], 0.0)
            result[part, head] = kept.astype(BF16)
        other_result(head).start()
        own_result(head).start()
        return carry

    lax.fori_loop(0, OWN, attend, 0, unroll=True)

    for head in range(OWN):
        span = pl.ds(pl.multiple_of((other * OWN + head) * HD, HD), HD)
        arrived = out_ref.at[:, span]
        remote(arrived, arrived, send_o.at[head], recv_o.at[head], sibling).wait_recv()
        other_result(head).wait_send()
        own_result(head).wait()

    for copy in param_copies + [sums_copy, shared] + sum_copies:
        copy.wait_send()

    def sent(step, carry):
        @pl.when((chip + step) % PLANE < UNITS)
        def _():
            remote(source_of(0), landing, send_a.at[step], recv_a.at[chip], partner).wait_send()

        return carry

    lax.fori_loop(1, PLANE, sent, 0)

    @pl.when(owner)
    def _():
        for index in range(GROUPS):
            to_sibling(index).wait_send()
            to_neighbour(index).wait_send()
            passed_on(index).wait_send()

        def sent_block(target, carry):
            @pl.when(plane_device(core * CLIPS_HERE + target, unit_core)[0] != s)
            def _():
                remote(
                    sending.at[target, pl.ds(0, WIRE)],
                    units.at[unit_slot, pl.ds(0, WIRE)],
                    send_c.at[target],
                    recv_c.at[unit_slot],
                    partner,
                ).wait_send()

            return carry

        lax.fori_loop(0, CLIPS_HERE, sent_block, 0)


def shards(
    patches,
    clip_shape,
    shard_counts,
    patch_weight,
    patch_bias,
    time_mod,
    block_mod,
    w_query,
    query_bias,
    w_keyvalue,
    keyvalue_bias,
    norm_gain,
):
    smem = pl.BlockSpec(memory_space=pltpu.SMEM)
    anywhere = pl.BlockSpec(memory_space=pl.ANY)
    dma = pltpu.SemaphoreType.DMA
    return pl.pallas_call(
        kernel,
        out_shape=jax.ShapeDtypeStruct((TOK, HALF), BF16),
        in_specs=[smem, smem] + [anywhere] * 10,
        out_specs=anywhere,
        scratch_shapes=[
            pltpu.VMEM((20, HALF), BF16),
            pltpu.VMEM((20, D), BF16),
            pltpu.VMEM((1, HALF), F32),
            pltpu.VMEM((1, D), F32),
            pltpu.VMEM((2, HALF), F32),
            pltpu.VMEM((5, 4, HALF + D), BF16),
            pltpu.VMEM((2, CIN, TOK), BF16),
            pltpu.VMEM((2, 2, CIN // 2, HALF), BF16),
            pltpu.VMEM((2, 1, HALF), F32),
            pltpu.VMEM((2, 2, HALF), F32),
            pltpu.VMEM((2, CLIPS_HERE, 2, HALF), F32),
            pltpu.VMEM((CIN + 8, HD), F32),
            pltpu.VMEM((CIN + 8, HD), F32),
            pltpu.VMEM((CIN, HALF), F32),
            pltpu.VMEM((CLIPS_HERE * BLOCK, D), BF16),
            pltpu.VMEM((2, PLANE, 2, 5, 4, HD), BF16),
            pltpu.VMEM((D, HD), BF16),
            pltpu.VMEM((CLIPS_HERE, BLOCK, HD), BF16),
            pltpu.VMEM((3 * OWN, HD, HD), BF16),
            pltpu.VMEM((2 * TOK, HD), BF16),
            pltpu.VMEM((2 * TOK, HD), F32),
            pltpu.VMEM((2 * TOK, HD), F32),
            pltpu.VMEM((2 * TOK, HD), F32),
            pltpu.VMEM((OWN, 2 * TOK, HD), F32),
            pltpu.VMEM((OWN, 2 * TOK, HD), F32),
            pltpu.VMEM((OWN, 2 * TOK, 2 * HD), BF16),
            pltpu.VMEM((2 * TOK, HD), F32),
            pltpu.VMEM((2 * TOK, HD), F32),
            pltpu.VMEM((2 * TOK, HD), F32),
            pltpu.VMEM((8, 2 * TOK), F32),
            pltpu.VMEM((3, 8, 2 * TOK), F32),
            pltpu.VMEM((2, OWN, TOK, HD), BF16),
            dma((PLANE,)),
            dma((PLANE,)),
            dma((3 * GROUPS,)),
            dma((3 * GROUPS,)),
            dma((CLIPS_HERE,)),
            dma((3 * OWN,)),
            dma((7,)),
            dma((7,)),
            dma((3,)),
            dma((3,)),
            dma((OWN,)),
            dma((OWN,)),
            dma((11,)),
            dma((OWN,)),
        ],
        compiler_params=pltpu.CompilerParams(
            collective_id=0, has_side_effects=True, vmem_limit_bytes=60 << 20
        ),
    )(
        clip_shape.T,
        shard_counts,
        patches.T,
        patch_weight,
        patch_bias,
        block_mod,
        time_mod,
        w_query,
        w_keyvalue,
        query_bias,
        keyvalue_bias,
        norm_gain,
    )


def solution(mesh):
    return jax.shard_map(
        shards,
        mesh=mesh,
        in_specs=(
            P("seq", None),
            P(),
            P(),
            P(None, "mp"),
            P("mp"),
            P(None, None, "mp"),
            P(None, "mp"),
            P("seq", "mp"),
            P("mp"),
            P("seq", "mp"),
            P("mp"),
            P(None, "mp"),
        ),
        out_specs=P("seq", "mp"),
        check_vma=False,
    )
```

```python
import functools
import math

import jax
import jax.numpy as jnp
from jax import lax
from jax.experimental import pallas as pl
from jax.experimental.pallas import tpu as pltpu
from jax.sharding import PartitionSpec as P

D = 2560
HALF = D // 2
HEADS = 20
HD = 128
CIN = 64
CLIPS = 64
TOK = 256
PLANE = 32
CLIPS_HERE = 16
UNITS = 30
OWN = 5
GROUPS = 8
DIRECT = 5
BLOCK = 80
WIRE = 72
EPSILON = 1e-06
F32 = jnp.float32
BF16 = jnp.bfloat16
MESH = pl.DeviceIdType.MESH


def unit_target(unit):
    is_query = unit < HEADS // 2
    pair = unit - HEADS // 2
    head = jnp.where(is_query, unit, pair // 2)
    core = head // OWN
    slot = head % OWN + jnp.where(is_query, 0, OWN + OWN * (pair % 2))
    return core, slot


def kernel(
    shape_hbm,
    counts_hbm,
    patches_ref,
    weight_ref,
    bias_ref,
    block_ref,
    time_ref,
    query_weight_ref,
    pair_weight_ref,
    query_bias_hbm,
    pair_bias_hbm,
    gain_hbm,
    out_ref,
    shape_ref,
    counts_ref,
    query_weight,
    pair_weight,
    query_bias_ref,
    pair_bias_ref,
    gain_ref,
    rows_ref,
    tokens,
    weight_all,
    bias_all,
    block_all,
    time_all,
    row_sums,
    row_sums_in,
    centred,
    modulated,
    clip_rows,
    landed,
    columns,
    partial,
    sending,
    units,
    rows_aug,
    scale_rows,
    cosines,
    sines,
    query_rows,
    key_rows,
    value_rows,
    valid_rows,
    query_acc,
    key_acc,
    sums_out,
    sums_in,
    result,
    send_a,
    recv_a,
    send_b,
    recv_b,
    send_c,
    recv_c,
    send_p,
    recv_p,
    send_s,
    recv_s,
    send_o,
    recv_o,
    local,
    local_o,
):
    s = lax.axis_index("seq")
    m = lax.axis_index("mp")
    x_lo = s // (2 * PLANE)
    chip = (s // 2) % PLANE
    core = s % 2
    other = 1 - core
    owner = chip < UNITS
    unit_core, unit_slot = unit_target(chip)
    crossing = jnp.logical_and(owner, unit_core != core)

    def plane_device(index, side):
        return (x_lo * 2 * PLANE + index * 2 + side, m)

    sibling = plane_device(chip, other)
    partner = (s, 1 - m)
    diagonal = (sibling[0], 1 - m)
    neighbour = (s + 2 * PLANE * (1 - 2 * x_lo), m)
    adjacent = (neighbour[0], 1 - m)
    across = (neighbour[0] - core + other, m)

    def remote(src, dst, send, recv, device):
        return pltpu.make_async_remote_copy(
            src_ref=src, dst_ref=dst, send_sem=send, recv_sem=recv, device_id=device, device_id_type=MESH
        )

    barrier = pltpu.get_barrier_semaphore()

    def far_first(index):
        return PLANE // 2 + (1 - 2 * (index % 2)) * ((index + 1) // 2)

    def greet(index, carry):
        step = far_first(index)
        pl.semaphore_signal(
            barrier, inc=1, device_id=plane_device((chip + step) % PLANE, core), device_id_type=MESH
        )
        return carry

    lax.fori_loop(0, PLANE - 1, greet, 0)
    for device in (neighbour, across, adjacent, partner, diagonal, sibling):
        pl.semaphore_signal(barrier, inc=1, device_id=device, device_id_type=MESH)

    @pl.when(chip // CLIPS_HERE != core)
    def _():
        def greet_owner(step, carry):
            unit = jnp.where(
                step < OWN, core * OWN + step, HEADS // 2 + core * 2 * OWN + step - OWN
            )
            pl.semaphore_signal(
                barrier, inc=1, device_id=plane_device(unit, other), device_id_type=MESH
            )
            return carry

        lax.fori_loop(0, 3 * OWN, greet_owner, 0)

    half_rows = pl.ds(pl.multiple_of(core * (CIN // 2), CIN // 2), CIN // 2)
    own_clips = pl.ds(x_lo * PLANE + core * CLIPS_HERE, CLIPS_HERE)
    adjacent_clips = pl.ds((1 - x_lo) * PLANE + core * CLIPS_HERE, CLIPS_HERE)

    weight_copies = [
        pltpu.make_async_copy(shape_hbm, shape_ref, local.at[11]),
        pltpu.make_async_copy(counts_hbm, counts_ref, local.at[12]),
        pltpu.make_async_copy(query_weight_ref, query_weight, local.at[0]),
        pltpu.make_async_copy(pair_weight_ref, pair_weight, local.at[1]),
    ]
    own_copies = [
        pltpu.make_async_copy(patches_ref, tokens.at[core], local.at[2]),
        pltpu.make_async_copy(weight_ref.at[pl.ds(0, CIN // 2)], weight_all.at[m, 0], local.at[3]),
        pltpu.make_async_copy(
            weight_ref.at[pl.ds(CIN // 2, CIN // 2)], weight_all.at[m, 1], local.at[4]
        ),
        pltpu.make_async_copy(bias_ref, bias_all.at[m, 0], local.at[5]),
        pltpu.make_async_copy(block_ref, block_all.at[m], local.at[6]),
        pltpu.make_async_copy(time_ref.at[own_clips], time_all.at[m], local.at[7]),
        pltpu.make_async_copy(query_bias_hbm, query_bias_ref.at[0], local.at[8]),
        pltpu.make_async_copy(pair_bias_hbm, pair_bias_ref.at[0], local.at[9]),
        pltpu.make_async_copy(gain_hbm, gain_ref, local.at[10]),
    ]
    for copy in weight_copies + own_copies:
        copy.start()

    units[:, WIRE:, :] = jnp.zeros((3 * OWN, HD - WIRE, HD), BF16)
    rows_aug[:, CIN:] = jnp.where(
        lax.broadcasted_iota(jnp.int32, (2 * TOK, HD - CIN), 1) < 2, 1.0, 0.0
    ).astype(BF16)
    for copy in weight_copies:
        copy.wait()
    rows_ref[:, :, :HALF] = query_weight[...].reshape(5, 4, HALF)
    rows_ref[:, :, HALF:] = pair_weight[...].reshape(5, 4, D)

    clip = s // 2
    height = shape_ref[1, clip].astype(F32)
    width = shape_ref[2, clip].astype(F32)
    lane = lax.broadcasted_iota(jnp.int32, (1, HD), 1)
    other_pairs = HD // 6
    frame_pairs = HD // 2 - 2 * other_pairs
    pair_id = lane // 2
    in_frame = pair_id < frame_pairs
    in_row = jnp.logical_and(pair_id >= frame_pairs, pair_id < frame_pairs + other_pairs)
    within = jnp.where(
        in_frame,
        pair_id,
        jnp.where(in_row, pair_id - frame_pairs, pair_id - frame_pairs - other_pairs),
    ).astype(F32)
    axis_span = jnp.where(in_frame, 2.0 * frame_pairs, 2.0 * other_pairs).astype(F32)
    inverse = jnp.exp(-(2.0 * within / axis_span) * math.log(10000.0))
    even = lane % 2 == 0
    for part in range(2):
        slot = lax.broadcasted_iota(jnp.int32, (TOK, HD), 0)
        offset = counts_ref[2 * clip] if part else 0
        position = (slot + offset).astype(F32)
        line = jnp.floor((position + 0.5) / width)
        column_pos = position - line * width
        frame_pos = jnp.floor((line + 0.5) / height)
        row_pos = line - frame_pos * height
        angles = jnp.where(in_frame, frame_pos, jnp.where(in_row, row_pos, column_pos)) * inverse
        sine = jnp.sin(angles)
        cosines[part * TOK : (part + 1) * TOK, :] = jnp.cos(angles)
        sines[part * TOK : (part + 1) * TOK, :] = jnp.where(even, -sine, sine)
        valid = slot < counts_ref[2 * clip + part]
        kept = jnp.where(valid, 1.0, 0.0).astype(BF16)
        valid_rows[part * TOK : (part + 1) * TOK, :] = jnp.where(valid, 1.0, 0.0)
        for head in range(OWN):
            value_rows[head, part * TOK : (part + 1) * TOK, HD:] = kept

    for copy in own_copies:
        copy.wait()
    for part in range(2):
        block_rows = slice(part * CIN // 2, (part + 1) * CIN // 2)
        row_sums[block_rows, :] = jnp.broadcast_to(
            jnp.sum(weight_all[m, part].astype(F32), axis=1, keepdims=True), (CIN // 2, HD)
        )
    row_sums[CIN:, :] = jnp.broadcast_to(jnp.sum(bias_all[m], axis=1, keepdims=True), (8, HD))

    pl.semaphore_wait(barrier, PLANE - 1 + 6 + jnp.where(crossing, CLIPS_HERE, 0))

    param_copies = [
        remote(patches_ref, tokens.at[core], send_p.at[0], recv_p.at[0], sibling),
        remote(weight_ref.at[half_rows], weight_all.at[m, core], send_p.at[1], recv_p.at[1], adjacent),
        remote(bias_ref, bias_all.at[m, 0], send_p.at[2], recv_p.at[2], adjacent),
        remote(block_ref, block_all.at[m], send_p.at[3], recv_p.at[3], adjacent),
        remote(time_ref.at[adjacent_clips], time_all.at[m], send_p.at[4], recv_p.at[4], adjacent),
    ]
    sums_copy = remote(row_sums, row_sums_in, send_p.at[6], recv_p.at[6], adjacent)
    sums_copy.start()
    for copy in param_copies:
        copy.start()

    def source_of(unit):
        return rows_ref.at[:, :, pl.ds(pl.multiple_of(unit * HD, HD), HD)]

    landing = landed.at[x_lo, chip, core]

    def scatter(index, carry):
        step = far_first(index)
        unit = (chip + step) % PLANE

        @pl.when(unit < UNITS)
        def _():
            remote(
                source_of(unit), landing, send_a.at[step], recv_a.at[chip], plane_device(unit, core)
            ).start()

        return carry

    lax.fori_loop(0, PLANE - 1, scatter, 0)

    @pl.when(owner)
    def _():
        pltpu.make_async_copy(source_of(chip), landing, recv_a.at[chip]).start()

    depth = chip // 4

    def group_of(index):
        return pl.ds((depth + (0, 1, 7, 2, 6, 3, 5, 4)[index]) % GROUPS * 4, 4)

    def to_sibling(index):
        block = landed.at[x_lo, group_of(index), core]
        return remote(block, block, send_b.at[index], recv_b.at[index], sibling)

    def to_neighbour(index):
        block = landed.at[x_lo, group_of(index), core]
        slot = GROUPS + index
        return remote(block, block, send_b.at[slot], recv_b.at[slot], neighbour)

    def passed_on(index):
        block = landed.at[1 - x_lo, group_of(index), core]
        slot = 2 * GROUPS + index
        return remote(block, block, send_b.at[slot], recv_b.at[slot], sibling)

    def to_across(index):
        block = landed.at[x_lo, group_of(index), core]
        slot = 2 * GROUPS + index
        return remote(block, block, send_b.at[slot], recv_b.at[slot], across)

    def from_across(index):
        block = landed.at[1 - x_lo, group_of(index), other]
        slot = 2 * GROUPS + index
        return remote(block, block, send_b.at[slot], recv_b.at[slot], sibling)

    def hand_on(groups):
        @pl.when(owner)
        def _():
            for index in groups:
                first = (depth + (0, 1, 7, 2, 6, 3, 5, 4)[index]) % GROUPS * 4
                for step in range(4):
                    block = landed.at[x_lo, first + step, core]
                    pltpu.make_async_copy(block, block, recv_a.at[first + step]).wait()
                to_neighbour(index).start()
                if index >= DIRECT:
                    to_across(index).start()
                to_sibling(index).start()

    def modulate_half(half):
        mean = (row_sums[:, 0:1] + row_sums_in[:, 0:1]) / D
        centred[...] = weight_all[half].reshape(CIN, HALF).astype(F32) - mean[:CIN]
        bias_row = bias_all[half] - mean[CIN : CIN + 1]
        span = pl.ds(pl.multiple_of(half * HALF, HALF), HALF)

        def modulate(step, carry):
            rows = pl.multiple_of(step * CIN, CIN)
            scale = 1.0 + time_all[half, step, 1:2, :] + block_all[half, 1:2, :]
            modulated[pl.ds(rows, CIN), span] = (centred[...] * scale).astype(BF16)
            clip_rows[0, pl.ds(step, 1), :] = bias_row * scale
            clip_rows[1, pl.ds(step, 1), :] = time_all[half, step, 0:1, :] + block_all[half, 0:1, :]
            return carry

        lax.fori_loop(0, CLIPS_HERE, modulate, 0)
        for kind in range(2):
            high = clip_rows[kind].astype(BF16)
            low = (clip_rows[kind] - high.astype(F32)).astype(BF16)
            base = CLIPS_HERE * (CIN + 2 * kind)
            modulated[base : base + CLIPS_HERE, span] = high
            modulated[base + CLIPS_HERE : base + 2 * CLIPS_HERE, span] = low

    hand_on(range(0, 3))
    sums_copy.wait_recv()
    modulate_half(m)
    hand_on(range(3, GROUPS))

    param_copies[1].wait_recv()
    weight_block = weight_all.at[1 - m, core]
    shared = remote(weight_block, weight_block, send_p.at[5], recv_p.at[5], sibling)
    shared.start()

    @pl.when(owner)
    def _():
        for index in range(DIRECT):
            to_neighbour(index).wait_recv()
            passed_on(index).start()

    for copy in param_copies[:1] + param_copies[2:] + [shared]:
        copy.wait_recv()
    modulate_half(1 - m)

    @pl.when(owner)
    def _():
        for index in range(GROUPS):
            to_sibling(index).wait_recv()
        columns[0] = landed[x_lo].reshape(HALF, HD)
        here_span = pl.ds(pl.multiple_of(x_lo * HALF, HALF), HALF)
        there_span = pl.ds(pl.multiple_of((1 - x_lo) * HALF, HALF), HALF)
        for turn in range(4):
            rows = slice(turn * 4 * CIN, (turn + 1) * 4 * CIN)
            partial[rows, :] = jnp.dot(
                modulated[rows, here_span], columns[0], preferred_element_type=F32
            )
        rows = slice(CLIPS_HERE * CIN, CLIPS_HERE * (CIN + 4))
        partial[rows, :] = jnp.dot(
            modulated[rows, here_span], columns[0], preferred_element_type=F32
        )
        for index in range(GROUPS):
            if index >= DIRECT:
                to_neighbour(index).wait_recv()
            from_across(index).wait_recv()
        columns[1] = landed[1 - x_lo].reshape(HALF, HD)
        extra = partial[rows, :] + jnp.dot(
            modulated[rows, there_span], columns[1], preferred_element_type=F32
        )
        bias_rows = extra[:CLIPS_HERE] + extra[CLIPS_HERE : 2 * CLIPS_HERE]
        shift_rows = extra[2 * CLIPS_HERE : 3 * CLIPS_HERE] + extra[3 * CLIPS_HERE :]
        bias_low = bias_rows - bias_rows.astype(BF16).astype(F32)
        shift_low = shift_rows - shift_rows.astype(BF16).astype(F32)
        index = lax.broadcasted_iota(jnp.int32, (BLOCK - CIN, HD), 0)
        for target in range(CLIPS_HERE):
            row = slice(target, target + 1)
            tail = jnp.where(
                index == 0,
                bias_rows[row],
                jnp.where(
                    index == 1,
                    bias_low[row],
                    jnp.where(
                        index == 2, shift_rows[row], jnp.where(index == 3, shift_low[row], 0.0)
                    ),
                ),
            )
            sending[target, CIN:, :] = tail.astype(BF16)
        ahead = (core * 4 - depth) % GROUPS
        backward = jnp.logical_or(ahead <= 2, ahead == 7)
        for turn in range(4):
            chunk = jnp.where(backward, 3 - turn, turn)
            span = pl.ds(pl.multiple_of(chunk * 4 * CIN, 4 * CIN), 4 * CIN)
            folded = partial[span, :] + jnp.dot(
                modulated[span, there_span], columns[1], preferred_element_type=F32
            )
            for piece in range(4):
                sending[chunk * 4 + piece, 0:CIN, :] = folded[piece * CIN : (piece + 1) * CIN].astype(BF16)

            for piece in range(4):
                target = chunk * 4 + (piece + chip // 4) % 4
                device = plane_device(core * CLIPS_HERE + target, unit_core)

                @pl.when(device[0] != s)
                def _():
                    remote(
                        sending.at[target, pl.ds(0, WIRE)],
                        units.at[unit_slot, pl.ds(0, WIRE)],
                        send_c.at[target],
                        recv_c.at[unit_slot],
                        device,
                    ).start()

                @pl.when(device[0] == s)
                def _():
                    pltpu.make_async_copy(
                        sending.at[target, pl.ds(0, WIRE)], units.at[unit_slot, pl.ds(0, WIRE)], recv_c.at[unit_slot]
                    ).start()


    for part in range(2):
        rows_aug[part * TOK : (part + 1) * TOK, 0:CIN] = tokens[part].T

    def statistics(step, carry):
        rows = pl.ds(pl.multiple_of(step * 128, 128), 128)
        patch = rows_aug[rows, 0:CIN]
        total = jnp.zeros((128, 1), F32)
        square = jnp.zeros((128, 1), F32)
        for half in range(2):
            embedded = (
                jnp.dot(patch, weight_all[half].reshape(CIN, HALF), preferred_element_type=F32)
                + bias_all[half]
            )
            total += jnp.sum(embedded, axis=1, keepdims=True)
            square += jnp.sum(embedded * embedded, axis=1, keepdims=True)
        average = total / D
        variance = square / D - average * average
        scale_rows[rows, :] = jnp.broadcast_to(lax.rsqrt(variance + EPSILON), (128, HD))
        return carry

    lax.fori_loop(0, 4, statistics, 0)

    def collect(slot, carry):
        block = units.at[slot, pl.ds(0, WIRE)]
        pltpu.make_async_copy(block, block, recv_c.at[slot]).wait()
        return carry

    query_acc[...] = jnp.zeros_like(query_acc)
    key_acc[...] = jnp.zeros_like(key_acc)

    def unit_rows(slot):
        unit = units[slot]
        shift_row = unit[CIN + 2 : CIN + 3].astype(F32) + unit[CIN + 3 : CIN + 4].astype(F32)
        return unit, shift_row

    def rotated(values, rows):
        partner_rows = jnp.where(even, pltpu.roll(values, HD - 1, 1), pltpu.roll(values, 1, 1))
        return values * cosines[rows, :] + partner_rows * sines[rows, :]

    lax.fori_loop(0, 2 * OWN, collect, 0)

    def project(head, carry):
        column = pl.multiple_of((core * OWN + head) * HD, HD)
        query_unit, query_shift = unit_rows(head)
        key_unit, key_shift = unit_rows(OWN + head)
        both = jnp.concatenate([query_unit, key_unit], axis=1)
        query_shift += query_bias_ref[0:1, pl.ds(column, HD)]
        key_shift += pair_bias_ref[0:1, pl.ds(pl.multiple_of(column * 2, HD), HD)]
        for part in range(2):
            rows = slice(part * TOK, (part + 1) * TOK)
            product = jnp.dot(rows_aug[rows, :], both, preferred_element_type=F32)
            scale = scale_rows[rows, :]
            raw = product[:, :HD] * scale + query_shift
            query_acc[rows, :] += raw * raw
            query_rows[head, rows, :] = raw
            raw = product[:, HD:] * scale + key_shift
            key_acc[rows, :] += raw * raw
            key_rows[head, rows, :] = raw
        return carry

    lax.fori_loop(0, OWN, project, 0)

    ones = jnp.ones((16, 2 * HD), BF16)
    contract_lanes = (((1,), (1,)), ((), ()))
    contract_rows = (((0,), (0,)), ((), ()))

    def split_sums(values):
        high = values.astype(BF16)
        low = (values - high.astype(F32)).astype(BF16)
        both = jnp.concatenate([high, low], axis=1)
        return lax.dot_general(ones, both, contract_lanes, preferred_element_type=F32)[:8]

    def split_columns(row):
        high = row.astype(BF16).astype(F32)
        middle = (row - high).astype(BF16).astype(F32)
        low = row - high - middle
        index = lax.broadcasted_iota(jnp.int32, (16, 2 * TOK), 0)
        parts = jnp.where(
            index == 0, high, jnp.where(index == 1, middle, jnp.where(index == 2, low, 0.0))
        ).astype(BF16)
        return lax.dot_general(parts, ones[:, :HD], contract_rows, preferred_element_type=F32)

    query_sums = split_sums(query_acc[...])
    key_sums = split_sums(key_acc[...])
    sum_index = lax.broadcasted_iota(jnp.int32, (8, 2 * TOK), 0)
    sums_out[...] = jnp.where(sum_index == 0, query_sums, key_sums)
    sum_copies = [
        remote(sums_out, sums_in.at[0], send_s.at[0], recv_s.at[0], sibling),
        remote(sums_out, sums_in.at[1], send_s.at[1], recv_s.at[1], partner),
        remote(
            sums_out,
            sums_in.at[2],
            send_s.at[2],
            recv_s.at[2],
            diagonal,
        ),
    ]
    for copy in sum_copies:
        copy.start()

    def rotate(head, carry):
        column = pl.multiple_of((core * OWN + head) * HD, HD)
        query_gain = gain_ref[0:1, pl.ds(column, HD)]
        key_gain = gain_ref[1:2, pl.ds(column, HD)]
        for part in range(2):
            rows = slice(part * TOK, (part + 1) * TOK)
            query_rows[head, rows, :] = rotated(query_rows[head, rows, :] * query_gain, rows)
            key_rows[head, rows, :] = rotated(key_rows[head, rows, :] * key_gain, rows)
        return carry

    lax.fori_loop(0, OWN, rotate, 0)

    def collect_value(head, carry):
        return collect(2 * OWN + head, carry)

    lax.fori_loop(0, OWN, collect_value, 0)

    def values(head, carry):
        column = pl.multiple_of(((core * OWN + head) * 2 + 1) * HD, HD)
        unit, shift = unit_rows(2 * OWN + head)
        shift += pair_bias_ref[0:1, pl.ds(column, HD)]
        for part in range(2):
            rows = slice(part * TOK, (part + 1) * TOK)
            product = jnp.dot(rows_aug[rows, :], unit, preferred_element_type=F32)
            raw = product * scale_rows[rows, :] + shift
            value_rows[head, rows, :HD] = jnp.where(valid_rows[rows, :] > 0.0, raw, 0.0).astype(BF16)
        return carry

    lax.fori_loop(0, OWN, values, 0)

    for copy in sum_copies:
        copy.wait_recv()
    square_sums = sums_out[...] + sums_in[0] + sums_in[1] + sums_in[2]
    factors = lax.rsqrt(square_sums / (HEADS * HD) + EPSILON)
    query_factor = split_columns(factors[0:1] * (HD**-0.5 * math.log2(math.e)))
    key_factor = split_columns(factors[1:2])
    query_acc[...] = query_factor
    key_acc[...] = jnp.where(valid_rows[...] > 0.0, key_factor, 0.0)

    def own_result(head):
        span = pl.ds(pl.multiple_of((core * OWN + head) * HD, HD), HD)
        return pltpu.make_async_copy(result.at[core, head], out_ref.at[:, span], local_o.at[head])

    def other_result(head):
        span = pl.ds(pl.multiple_of((core * OWN + head) * HD, HD), HD)
        return remote(
            result.at[other, head], out_ref.at[:, span], send_o.at[head], recv_o.at[head], sibling
        )

    def attend(head, carry):
        keys = (key_rows[head] * key_acc[...]).astype(BF16)
        for part in (other, core):
            rows = pl.ds(pl.multiple_of(part * TOK, TOK), TOK)
            queries = (query_rows[head, rows, :] * query_acc[rows, :]).astype(BF16)
            scores = lax.dot_general(queries, keys, contract_lanes, preferred_element_type=F32)
            weights = jnp.exp2(scores).astype(BF16)
            summed = jnp.dot(weights, value_rows[head], preferred_element_type=F32)
            kept = jnp.where(valid_rows[rows, :] > 0.0, summed[:, :HD] / summed[:, HD:], 0.0)
            result[part, head] = kept.astype(BF16)
            if part is other:
                other_result(head).start()
        own_result(head).start()
        return carry

    lax.fori_loop(0, OWN, attend, 0, unroll=True)

    for head in range(OWN):
        span = pl.ds(pl.multiple_of((other * OWN + head) * HD, HD), HD)
        arrived = out_ref.at[:, span]
        remote(arrived, arrived, send_o.at[head], recv_o.at[head], sibling).wait_recv()
        other_result(head).wait_send()
        own_result(head).wait()

    for copy in param_copies + [sums_copy, shared] + sum_copies:
        copy.wait_send()

    def sent(step, carry):
        @pl.when((chip + step) % PLANE < UNITS)
        def _():
            remote(source_of(0), landing, send_a.at[step], recv_a.at[chip], partner).wait_send()

        return carry

    lax.fori_loop(1, PLANE, sent, 0)

    @pl.when(owner)
    def _():
        for index in range(GROUPS):
            to_sibling(index).wait_send()
            to_neighbour(index).wait_send()
            passed_on(index).wait_send()

        def sent_block(target, carry):
            @pl.when(plane_device(core * CLIPS_HERE + target, unit_core)[0] != s)
            def _():
                remote(
                    sending.at[target, pl.ds(0, WIRE)],
                    units.at[unit_slot, pl.ds(0, WIRE)],
                    send_c.at[target],
                    recv_c.at[unit_slot],
                    partner,
                ).wait_send()

            return carry

        lax.fori_loop(0, CLIPS_HERE, sent_block, 0)


def shards(
    patches,
    clip_shape,
    shard_counts,
    patch_weight,
    patch_bias,
    time_mod,
    block_mod,
    w_query,
    query_bias,
    w_keyvalue,
    keyvalue_bias,
    norm_gain,
):
    anywhere = pl.BlockSpec(memory_space=pl.ANY)
    dma = pltpu.SemaphoreType.DMA
    return pl.pallas_call(
        kernel,
        out_shape=jax.ShapeDtypeStruct((TOK, HALF), BF16),
        in_specs=[pl.BlockSpec(memory_space=pltpu.HBM)] * 12,
        out_specs=anywhere,
        scratch_shapes=[
            pltpu.SMEM((3, CLIPS), jnp.int32),
            pltpu.SMEM((2 * CLIPS,), jnp.int32),
            pltpu.VMEM((20, HALF), BF16),
            pltpu.VMEM((20, D), BF16),
            pltpu.VMEM((1, HALF), F32),
            pltpu.VMEM((1, D), F32),
            pltpu.VMEM((2, HALF), F32),
            pltpu.VMEM((5, 4, HALF + D), BF16),
            pltpu.VMEM((2, CIN, TOK), BF16),
            pltpu.VMEM((2, 2, CIN // 2, HALF), BF16),
            pltpu.VMEM((2, 1, HALF), F32),
            pltpu.VMEM((2, 2, HALF), F32),
            pltpu.VMEM((2, CLIPS_HERE, 2, HALF), F32),
            pltpu.VMEM((CIN + 8, HD), F32),
            pltpu.VMEM((CIN + 8, HD), F32),
            pltpu.VMEM((CIN, HALF), F32),
            pltpu.VMEM((CLIPS_HERE * (CIN + 4), D), BF16),
            pltpu.VMEM((2, CLIPS_HERE, HALF), F32),
            pltpu.VMEM((2, PLANE, 2, 5, 4, HD), BF16),
            pltpu.VMEM((2, HALF, HD), BF16),
            pltpu.VMEM((CLIPS_HERE * (CIN + 4), HD), F32),
            pltpu.VMEM((CLIPS_HERE, BLOCK, HD), BF16),
            pltpu.VMEM((3 * OWN, HD, HD), BF16),
            pltpu.VMEM((2 * TOK, HD), BF16),
            pltpu.VMEM((2 * TOK, HD), F32),
            pltpu.VMEM((2 * TOK, HD), F32),
            pltpu.VMEM((2 * TOK, HD), F32),
            pltpu.VMEM((OWN, 2 * TOK, HD), F32),
            pltpu.VMEM((OWN, 2 * TOK, HD), F32),
            pltpu.VMEM((OWN, 2 * TOK, 2 * HD), BF16),
            pltpu.VMEM((2 * TOK, HD), F32),
            pltpu.VMEM((2 * TOK, HD), F32),
            pltpu.VMEM((2 * TOK, HD), F32),
            pltpu.VMEM((8, 2 * TOK), F32),
            pltpu.VMEM((3, 8, 2 * TOK), F32),
            pltpu.VMEM((2, OWN, TOK, HD), BF16),
            dma((PLANE,)),
            dma((PLANE,)),
            dma((3 * GROUPS,)),
            dma((3 * GROUPS,)),
            dma((CLIPS_HERE,)),
            dma((3 * OWN,)),
            dma((7,)),
            dma((7,)),
            dma((3,)),
            dma((3,)),
            dma((OWN,)),
            dma((OWN,)),
            dma((13,)),
            dma((OWN,)),
        ],
        compiler_params=pltpu.CompilerParams(
            collective_id=0, has_side_effects=True, vmem_limit_bytes=24 << 20
        ),
    )(
        *[
            pltpu.with_memory_space_constraint(value, pltpu.HBM)
            for value in (
                clip_shape.T,
                shard_counts,
                patches.T,
                patch_weight,
                patch_bias,
                block_mod,
                time_mod,
                w_query,
                w_keyvalue,
                query_bias,
                keyvalue_bias,
                norm_gain,
            )
        ]
    )


def solution(mesh):
    return jax.shard_map(
        shards,
        mesh=mesh,
        in_specs=(
            P("seq", None),
            P(),
            P(),
            P(None, "mp"),
            P("mp"),
            P(None, None, "mp"),
            P(None, "mp"),
            P("seq", "mp"),
            P("mp"),
            P("seq", "mp"),
            P("mp"),
            P(None, "mp"),
        ),
        out_specs=P("seq", "mp"),
        check_vma=False,
    )
```
